32 devices in a mesh: tract: 2 (over x), epoch: 16 (over z, y, core).
Axes of the slice: x: 2, y: 2, z: 4, core: 2. Of those that a mesh axis runs over, the one named last changes fastest.
Arguments:
- templates: bfloat16 [32, 64, 512], P(('tract', 'epoch')), parts along dimension 0, may hold values from -5 to 5
- epoch_patch: int32 [128], P(('tract', 'epoch')), parts along dimension 0, may hold values from 0 to 15, as said below
- images: bfloat16 [128, 64, 512], P(('tract', 'epoch')), parts along dimension 0, may hold values from -12 to 12
- good_pixels: int32 [128, 64, 512], P(('tract', 'epoch')), parts along dimension 0, may hold values 0 or 1
Outputs:
- difference_coadd: float32 [32, 64, 512], P(('tract', 'epoch')), parts along dimension 0
- kernel_coefs: float32 [128, 27], P(('tract', 'epoch')), parts along dimension 0
The draws below stay inside these ranges and needn't reach their ends.
There are 2 independent parts, one for each index of `tract`. The reference program is written for one: setup_inputs(seed, part) draws one part's arguments, and reference() takes and returns one part's arrays. A program takes and returns all parts, laid end to end along the dimension named above; each array names one. Nothing has to cross between parts.
Inputs may be any that keep to these rules, and one draw needn't show every extreme that they name: `epoch_patch`: epoch e is held by the device of index e // 4 along the epoch axis, and its patch p, held by the device of index p, lies within 4 of that index.
All inputs are finite; a program needn't handle non-finite values. No bound on the sum of `good_pixels` on one device may be relied on, other than what follows from the above.
Results may differ from the reference program's by a relative error of at most 0.0045.
The reference program's roundings to bfloat16 on the way count: a program that leaves them out, or rounds other values in their place, can miss the bound.
Values may be sent and summed in bfloat16 or wider, within the bound.
No kernel may reach another device: no remote copies, remote signals or barrier semaphores. Data moves between devices by JAX's collectives and lax.ppermute only.
A program may use at most 64 MiB of HBM per device.

```python
import math
from functools import partial
import jax
import jax.numpy as jnp
from jax import lax

ROWS = 64
COLS = 512
E_DEV = 4
RADIUS = 4
KHALF = 9
NBASIS = 27
NPATCH = 16
NEPOCHS = 64


def patch_list(key):
    offsets = jax.random.randint(jax.random.fold_in(key, 101), (NPATCH, E_DEV), -RADIUS, RADIUS + 1)
    owners = jnp.arange(NPATCH, dtype=jnp.int32)[:, None]
    patches = jnp.clip(owners + offsets, 0, NPATCH - 1)
    patches = patches.at[RADIUS, 0].set(0)
    patches = patches.at[NPATCH - 1 - RADIUS, 1].set(NPATCH - 1)
    return patches.reshape(NEPOCHS).astype(jnp.int32)


def template_field(key):
    rough_part = jax.random.normal(jax.random.fold_in(key, 202), (NPATCH, ROWS, COLS), jnp.float32)
    return jnp.clip(rough_part, -5.0, 5.0)


def blur_once(source, profile):
    padded = jnp.pad(source, ((KHALF, KHALF), (KHALF, KHALF)))
    across = jnp.zeros((ROWS, COLS), jnp.float32)
    for offset in range(-KHALF, KHALF + 1):
        across = across + profile[offset + KHALF] * padded[KHALF:KHALF + ROWS, KHALF - offset:KHALF - offset + COLS]
    padded = jnp.pad(across, ((KHALF, KHALF), (0, 0)))
    result = jnp.zeros((ROWS, COLS), jnp.float32)
    for offset in range(-KHALF, KHALF + 1):
        result = result + profile[offset + KHALF] * padded[KHALF - offset:KHALF - offset + ROWS, :]
    return result


def draw_templates(key, part):
    return template_field(key).astype(jnp.bfloat16)


def draw_epoch_patch(key, part):
    return patch_list(key)


def draw_images(key, part):
    template_grid = template_field(key)
    patches = patch_list(key)
    widths = jnp.exp(jax.random.uniform(jax.random.fold_in(key, 301), (NEPOCHS,), jnp.float32, math.log(1.2), math.log(3.0)))
    fluxes = jax.random.uniform(jax.random.fold_in(key, 302), (NEPOCHS,), jnp.float32, 0.5, 2.0)
    places = jnp.arange(-KHALF, KHALF + 1).astype(jnp.float32)

    def render(record):
        patch_index, blur_width, brightness = record
        profile = jnp.exp(-places * places / (2.0 * blur_width * blur_width))
        profile = profile / jnp.sqrt(jnp.sum(profile * profile))
        source = lax.dynamic_index_in_dim(template_grid, patch_index, 0, keepdims=False)
        return brightness * blur_once(source, profile)
    blurred = lax.map(render, (patches, widths, fluxes))
    noise_field = 0.3 * jax.random.normal(jax.random.fold_in(key, 303), blurred.shape, jnp.float32)
    return jnp.clip(blurred + noise_field, -12.0, 12.0).astype(jnp.bfloat16)


def touch_ends(entries, rng, least, largest):
    index_at = [jax.random.randint(jax.random.fold_in(rng, axis), (), 0, length) for axis, length in enumerate(entries.shape)]
    main_axis = entries.shape.index(max(entries.shape))
    next_to = index_at[:main_axis] + [(index_at[main_axis] + 1) % entries.shape[main_axis]] + index_at[main_axis + 1:]
    return entries.at[tuple(index_at)].set(least).at[tuple(next_to)].set(largest)


def setup_inputs(seed: int = 0, part: int = 0) -> dict:
    key_of = jax.random.split(jax.random.key(seed), 5)
    own_keys = jax.random.split(jax.random.fold_in(key_of[4], part), 5)
    return {
        "templates": draw_templates(jax.random.fold_in(jax.random.fold_in(key_of[4], part), 71), part),
        "epoch_patch": draw_epoch_patch(jax.random.fold_in(jax.random.fold_in(key_of[4], part), 71), part),
        "images": draw_images(jax.random.fold_in(jax.random.fold_in(key_of[4], part), 71), part),
        "good_pixels": touch_ends((jax.random.randint(own_keys[3], (NEPOCHS, ROWS, COLS), 0, 8) < 7).astype(jnp.int32), jax.random.fold_in(own_keys[3], 1), 0, 1),
    }


SIGMAS = (1.0, 2.0, 4.0)
RIDGE_TERM = 0.1

def kernel_taps():
    places = jnp.arange(-KHALF, KHALF + 1).astype(jnp.float32)
    profiles = []
    for spread in SIGMAS:
        for degree in range(3):
            profile = places ** degree * jnp.exp(-places * places / (2.0 * spread * spread))
            profiles.append(profile / jnp.sqrt(jnp.sum(profile * profile)))
    rounded = lax.optimization_barrier(jnp.stack(profiles).astype(jnp.bfloat16))
    return rounded.astype(jnp.float32)

def shift_columns(source, offset):
    padded = jnp.pad(source, ((0, 0), (KHALF, KHALF)))
    return padded[:, KHALF - offset:KHALF - offset + COLS]

def shift_rows(source, offset):
    padded = jnp.pad(source, ((0, 0), (KHALF, KHALF), (0, 0)))
    return padded[:, KHALF - offset:KHALF - offset + ROWS, :]

def basis_images(template, weights):
    column_stack = jnp.stack([shift_columns(template, offset) for offset in range(-KHALF, KHALF + 1)])
    smoothed = jnp.einsum('ku,uyx->kyx', weights, column_stack, precision=lax.Precision.HIGHEST)
    smoothed = lax.optimization_barrier(smoothed.astype(jnp.bfloat16)).astype(jnp.float32)
    row_stack = jnp.stack([shift_rows(smoothed, offset) for offset in range(-KHALF, KHALF + 1)])
    row_stack = row_stack.reshape(2 * KHALF + 1, 3, 3, ROWS, COLS)
    wide_rows = weights.reshape(3, 3, 2 * KHALF + 1)
    basis_set = jnp.einsum('sjv,vsiyx->sijyx', wide_rows, row_stack, precision=lax.Precision.HIGHEST)
    basis_set = lax.optimization_barrier(basis_set.astype(jnp.bfloat16)).astype(jnp.float32)
    return basis_set.reshape(NBASIS, ROWS * COLS)

def fit_one(templates_f, weights, record):
    science, good_mask, patch_index = record
    template = lax.dynamic_index_in_dim(templates_f, patch_index, 0, keepdims=False)
    basis_set = basis_images(template, weights)
    weight = good_mask.reshape(-1).astype(jnp.float32)
    pixels = science.reshape(-1).astype(jnp.float32)
    normal = jnp.einsum('kp,lp->kl', basis_set, basis_set * weight, precision=lax.Precision.HIGHEST)
    normal = normal / (ROWS * COLS) + RIDGE_TERM * jnp.eye(NBASIS, dtype=jnp.float32)
    target = jnp.einsum('kp,p->k', basis_set, weight * pixels, precision=lax.Precision.HIGHEST) / (ROWS * COLS)
    factor = jnp.linalg.cholesky(normal)
    coefficients = jax.scipy.linalg.cho_solve((factor, True), target)
    fitted = jnp.einsum('k,kp->p', coefficients, basis_set, precision=lax.Precision.HIGHEST)
    difference = weight * (pixels - fitted)
    return (coefficients, difference.reshape(ROWS, COLS))

def reference(templates, epoch_patch, images, good_pixels):
    weights = kernel_taps()
    templates_f = templates.astype(jnp.float32)
    coefficients, differences = lax.map(partial(fit_one, templates_f, weights), (images, good_pixels, epoch_patch))
    deep_sum = jax.ops.segment_sum(differences, epoch_patch, num_segments=NPATCH)
    return (deep_sum, coefficients)
```

```python
from functools import partial

import jax
import jax.numpy as jnp
import numpy as np
from jax import lax
from jax.experimental import pallas as pl
from jax.experimental.pallas import tpu as pltpu
from jax.sharding import PartitionSpec as P

RADIUS = 4
KHALF = 9
SIGMAS = (1.0, 2.0, 4.0)
DEGREES = 3
NBASIS = (len(SIGMAS) * DEGREES) * DEGREES
RIDGE_TERM = 0.1
AXIS = "epoch"
CORES = 2
REACH = RADIUS // CORES
LANES = 128
SUB = 8
TAPS = 2 * KHALF + 1
SLOT = 32


def kernel_taps():
    places = np.arange(-KHALF, KHALF + 1).astype(np.float64)
    profiles = []
    for spread in SIGMAS:
        for degree in range(DEGREES):
            profile = places**degree * np.exp(-places * places / (2.0 * spread * spread))
            profiles.append(profile / np.sqrt(np.sum(profile * profile)))
    return np.stack(profiles).astype(np.float32).astype(jnp.bfloat16)


def column_bands(taps):
    kernels = taps.shape[0]
    bands = np.zeros((2 * LANES, kernels, LANES), taps.dtype)
    for x in range(LANES):
        for tap in range(TAPS):
            bands[x + 2 * KHALF - tap, :, x] = taps[:, tap]
    return bands.reshape(2 * LANES, kernels * LANES)


def row_bands(taps, rows):
    bands = np.zeros((len(SIGMAS), rows // SUB, DEGREES, SUB, rows), taps.dtype)
    for y in range(rows):
        for tap in range(TAPS):
            source = y - tap + KHALF
            if 0 <= source < rows:
                bands[:, y // SUB, :, y % SUB, source] = taps[:, tap].reshape(len(SIGMAS), DEGREES)
    return bands.reshape(len(SIGMAS), rows * DEGREES, rows)


def split3(x):
    high = x.astype(jnp.bfloat16)
    rest = x - high.astype(jnp.float32)
    middle = rest.astype(jnp.bfloat16)
    low = (rest - middle.astype(jnp.float32)).astype(jnp.bfloat16)
    return high, middle, low


def fit_kernel(
    select_ref,
    own_ref,
    other_ref,
    near_ref,
    far_ref,
    swapped_near_ref,
    swapped_far_ref,
    images_ref,
    good_ref,
    column_ref,
    row_ref,
    coefs_ref,
    own_sum_ref,
    near_sum_ref,
    far_sum_ref,
    swap_sum_ref,
    window_ref,
    smooth_ref,
    basis_ref,
    sums_ref,
):
    epochs, rows, cols = images_ref.shape
    blocks = cols // LANES
    groups = rows // SUB
    planes = NBASIS + 1
    height = planes * SUB
    kernels = len(SIGMAS) * DEGREES
    f32, bf16 = jnp.float32, jnp.bfloat16

    sources = [
        own_ref.at[0],
        other_ref.at[0],
        near_ref.at[0],
        near_ref.at[1],
        far_ref.at[0],
        far_ref.at[1],
        swapped_near_ref.at[0],
        swapped_near_ref.at[1],
        swapped_far_ref.at[0],
        swapped_far_ref.at[1],
    ]
    lane = lax.broadcasted_iota(jnp.int32, (rows, cols + LANES), 1)
    inside = jnp.logical_and(lane >= KHALF, lane < cols + KHALF)
    for e in range(epochs):
        for index, source in enumerate(sources):

            @pl.when(select_ref[e] == index)
            def _():
                template = source[...].astype(f32)
                wide = jnp.concatenate([template, template[:, :LANES]], 1)
                wide = jnp.where(inside, pltpu.roll(wide, KHALF, 1), 0.0).astype(bf16)
                for b in range(blocks):
                    at = (e * blocks + b) * rows
                    window_ref[at : at + rows, :] = wide[:, b * LANES : (b + 2) * LANES]

    sums_ref[...] = jnp.zeros_like(sums_ref)

    for k in range(kernels):
        smooth_ref[:, k * LANES : (k + 1) * LANES] = jnp.dot(
            window_ref[...],
            column_ref[:, k * LANES : (k + 1) * LANES],
            preferred_element_type=f32,
        ).astype(bf16)

    row_a = lax.broadcasted_iota(jnp.int32, (height, height), 0)
    row_b = lax.broadcasted_iota(jnp.int32, (height, height), 1)
    same_row = row_a % SUB == row_b % SUB
    plane_of = lax.broadcasted_iota(jnp.int32, (height, LANES), 0) // SUB
    lane_of = lax.broadcasted_iota(jnp.int32, (height, LANES), 1)
    packed = jnp.zeros((height, LANES), f32)
    for e in range(epochs):
        for b in range(blocks):
            at = (e * blocks + b) * rows
            weight = good_ref[e, :, b * LANES : (b + 1) * LANES].astype(f32)
            image = images_ref[e, :, b * LANES : (b + 1) * LANES].astype(f32)
            out = [
                jnp.dot(
                    row_ref[s],
                    smooth_ref[at : at + rows, s * DEGREES * LANES : (s + 1) * DEGREES * LANES],
                    preferred_element_type=f32,
                )
                for s in range(len(SIGMAS))
            ]
            for g in range(groups):
                tiles = [
                    out[s][(g * DEGREES + j) * SUB : (g * DEGREES + j + 1) * SUB, i * LANES : (i + 1) * LANES]
                    for s in range(len(SIGMAS))
                    for i in range(DEGREES)
                    for j in range(DEGREES)
                ]
                mask = weight[g * SUB : (g + 1) * SUB]
                tiles = [tile * mask for tile in tiles + [image[g * SUB : (g + 1) * SUB]]]
                at_lane = g * cols + b * LANES
                basis_ref[e, :, at_lane : at_lane + LANES] = jnp.concatenate(tiles, 0).astype(bf16)
        basis = basis_ref[e]
        gram = lax.dot_general(
            basis, basis, (((1,), (1,)), ((), ())), preferred_element_type=f32
        )
        gram = jnp.where(same_row, gram, 0.0)
        place = (lane_of == plane_of + e * SLOT).astype(bf16)
        for part in split3(gram):
            packed = packed + jnp.dot(part, place, preferred_element_type=f32)
    fold = (
        lax.broadcasted_iota(jnp.int32, (SLOT, height), 0)
        == lax.broadcasted_iota(jnp.int32, (SLOT, height), 1) // SUB
    ).astype(bf16)
    system = jnp.zeros((SLOT, LANES), f32)
    for part in split3(packed):
        system = system + jnp.dot(fold, part, preferred_element_type=f32)
    plane = lax.broadcasted_iota(jnp.int32, (SLOT, LANES), 0)
    lane = lax.broadcasted_iota(jnp.int32, (SLOT, LANES), 1)
    slot = lane % SLOT
    system = system / (rows * cols) + jnp.where(plane == slot, RIDGE_TERM, 0.0)
    start = lane - slot
    for p in range(NBASIS):
        pivot_row = jnp.broadcast_to(system[p : p + 1], (SLOT, LANES))
        column = jnp.take_along_axis(system, start + p, axis=1)
        pivot = jnp.broadcast_to(column[p : p + 1], (SLOT, LANES))
        factor = jnp.where(plane == p, 0.0, column / pivot)
        system = system - factor * pivot_row
    diagonal = jnp.sum(jnp.where(plane == slot, system, 0.0), 0, keepdims=True)
    pivots = jnp.take_along_axis(
        jnp.broadcast_to(diagonal, (SLOT, LANES)), start + plane, axis=1
    )
    solved = jnp.take_along_axis(system, start + NBASIS, axis=1) / jnp.where(plane < NBASIS, pivots, 1.0)
    for e in range(epochs):
        column = jnp.broadcast_to(solved[:, e * SLOT : e * SLOT + 1], (SLOT, LANES))
        as_row = jnp.sum(jnp.where(plane == lane, column, 0.0), 0, keepdims=True)
        coefs_ref[e : e + 1, :] = as_row[:, :NBASIS]
        scale = [jnp.broadcast_to(column[k : k + 1], (SUB, LANES)) for k in range(NBASIS)]
        target = select_ref[e]
        for g in range(groups):
            for b in range(blocks):
                at_lane = g * cols + b * LANES
                tile = basis_ref[e, :, at_lane : at_lane + LANES].astype(f32)
                value = tile[NBASIS * SUB : planes * SUB]
                for k in range(NBASIS):
                    value = value - scale[k] * tile[k * SUB : (k + 1) * SUB]
                here = (target, slice(g * SUB, (g + 1) * SUB), slice(b * LANES, (b + 1) * LANES))
                sums_ref[here] = sums_ref[here] + value
    own_sum_ref[...] = sums_ref[0:2]
    near_sum_ref[...] = sums_ref[2:4]
    far_sum_ref[...] = sums_ref[4:6]
    swap_sum_ref[...] = sums_ref[6:10].astype(bf16)


def between_cores(block):
    n = lax.axis_size(AXIS)
    return lax.ppermute(block, AXIS, [(i, i ^ 1) for i in range(n)])


def between_chips(block, distance):
    chips = lax.axis_size(AXIS) // CORES
    route = []
    for chip in range(chips):
        for core in range(CORES):
            origin = chip + (distance if core == 0 else -distance)
            if 0 <= origin < chips:
                route.append((CORES * origin + core, CORES * chip + core))
            else:
                route.append((CORES * chip + 1 - core, CORES * chip + core))
    return lax.ppermute(block, AXIS, route)


def buffer_of(epoch_patch):
    device = lax.axis_index(AXIS)
    core = device % CORES
    chip_offset = epoch_patch // CORES - device // CORES
    same_core = epoch_patch % CORES == core
    side = jnp.where(core == 0, 1, -1)
    far = jnp.abs(chip_offset) - 1
    mine = 2 + 2 * far + jnp.where(same_core, 0, 1)
    theirs = 6 + 2 * far + jnp.where(same_core, 1, 0)
    away = jnp.where(chip_offset * side > 0, mine, theirs)
    return jnp.where(chip_offset == 0, jnp.where(same_core, 0, 1), away).astype(jnp.int32)


def shards(templates, epoch_patch, images, good_pixels):
    epochs, rows, cols = images.shape
    f32, bf16 = jnp.float32, jnp.bfloat16
    assert templates.shape[0] == 1 and epochs * SLOT <= LANES
    assert lax.axis_size(AXIS) % CORES == 0 and cols % LANES == 0 and rows % SUB == 0
    other = between_cores(templates)
    pair = jnp.concatenate([templates, other], 0)
    near, far = between_chips(pair, 1), between_chips(pair, 2)
    swapped_near, swapped_far = between_cores(near), between_cores(far)
    taps = kernel_taps()
    column = jnp.asarray(column_bands(taps))
    row = jnp.asarray(row_bands(taps, rows))
    height = (NBASIS + 1) * SUB
    tiles = epochs * (cols // LANES) * rows
    coefs, own_sum, near_sum, far_sum, swap_sum = pl.pallas_call(
        fit_kernel,
        out_shape=(
            jax.ShapeDtypeStruct((epochs, NBASIS), f32),
            jax.ShapeDtypeStruct((2, rows, cols), f32),
            jax.ShapeDtypeStruct((2, rows, cols), f32),
            jax.ShapeDtypeStruct((2, rows, cols), f32),
            jax.ShapeDtypeStruct((4, rows, cols), bf16),
        ),
        in_specs=[pl.BlockSpec(memory_space=pltpu.SMEM)]
        + [pl.BlockSpec(memory_space=pltpu.VMEM)] * 10,
        out_specs=[pl.BlockSpec(memory_space=pltpu.VMEM)] * 5,
        scratch_shapes=[
            pltpu.VMEM((tiles, 2 * LANES), bf16),
            pltpu.VMEM((tiles, column.shape[1]), bf16),
            pltpu.VMEM((epochs, height, rows // SUB * cols), bf16),
            pltpu.VMEM((10, rows, cols), f32),
        ],
        name="fit",
    )(
        buffer_of(epoch_patch),
        templates,
        other,
        near,
        far,
        swapped_near,
        swapped_far,
        images,
        good_pixels,
        column,
        row,
    )
    received = between_cores(swap_sum)
    near_sum = (near_sum + received[0:2].astype(f32)).astype(bf16)
    far_sum = (far_sum + received[2:4].astype(f32)).astype(bf16)
    near_back, far_back = between_chips(near_sum, -1), between_chips(far_sum, -2)
    total = own_sum + near_back.astype(f32) + far_back.astype(f32)
    deep_sum = total[0:1] + between_cores(total[1:2].astype(bf16)).astype(f32)
    return (deep_sum, coefs)


def solution(mesh):
    spec = P(("tract", AXIS), None, None)
    in_specs = (spec, P(("tract", AXIS)), spec, spec)
    out_specs = (spec, P(("tract", AXIS), None))
    return jax.shard_map(shards, mesh=mesh, in_specs=in_specs, out_specs=out_specs, check_vma=False)
```

```python
from functools import partial

import jax
import jax.numpy as jnp
import numpy as np
from jax import lax
from jax.experimental import pallas as pl
from jax.experimental.pallas import tpu as pltpu
from jax.sharding import PartitionSpec as P

RADIUS = 4
KHALF = 9
SIGMAS = (1.0, 2.0, 4.0)
DEGREES = 3
NBASIS = (len(SIGMAS) * DEGREES) * DEGREES
RIDGE_TERM = 0.1
AXIS = "epoch"
CORES = 2
REACH = RADIUS // CORES
LANES = 128
SUB = 8
TAPS = 2 * KHALF + 1
SLOT = 32


def kernel_taps():
    places = np.arange(-KHALF, KHALF + 1).astype(np.float64)
    profiles = []
    for spread in SIGMAS:
        for degree in range(DEGREES):
            profile = places**degree * np.exp(-places * places / (2.0 * spread * spread))
            profiles.append(profile / np.sqrt(np.sum(profile * profile)))
    return np.stack(profiles).astype(np.float32).astype(jnp.bfloat16)


def column_bands(taps):
    kernels = taps.shape[0]
    bands = np.zeros((2 * LANES, kernels, LANES), taps.dtype)
    for x in range(LANES):
        for tap in range(TAPS):
            bands[x + 2 * KHALF - tap, :, x] = taps[:, tap]
    return bands.reshape(2 * LANES, kernels * LANES)


def row_bands(taps, rows):
    bands = np.zeros((len(SIGMAS), rows // SUB, DEGREES, SUB, rows), taps.dtype)
    for y in range(rows):
        for tap in range(TAPS):
            source = y - tap + KHALF
            if 0 <= source < rows:
                bands[:, y // SUB, :, y % SUB, source] = taps[:, tap].reshape(len(SIGMAS), DEGREES)
    return bands.reshape(len(SIGMAS), rows * DEGREES, rows)


def split3(x):
    high = x.astype(jnp.bfloat16)
    rest = x - high.astype(jnp.float32)
    middle = rest.astype(jnp.bfloat16)
    low = (rest - middle.astype(jnp.float32)).astype(jnp.bfloat16)
    return high, middle, low


def plane_order():
    order = []
    n = DEGREES
    for s in range(len(SIGMAS)):
        at = s * n * n
        for i in range(n):
            order += [at + i * n, at + i * n + 1]
        order += [at + 2, at + n + 2]
    order += [s * n * n + 2 * n + 2 for s in range(len(SIGMAS))]
    return order + [NBASIS]


def plane_maps(epochs):
    order = plane_order()
    height = len(order) * SUB
    fold = np.zeros((SLOT, height), np.float32)
    place = np.zeros((epochs, height, LANES), np.float32)
    for position, k in enumerate(order):
        rows = slice(position * SUB, (position + 1) * SUB)
        fold[k, rows] = 1
        for e in range(epochs):
            place[e, rows, e * SLOT + k] = 1
    return fold.astype(jnp.bfloat16), place.reshape(epochs * height, LANES).astype(jnp.bfloat16)


def prepare_kernel(images_hbm, good_hbm, *refs):
    count = (len(refs) - 5) // 2
    images_ref, good_ref, semaphores = refs[-3:]
    masked_ref, weight_ref = refs[count : count + 2]
    moves = [(images_hbm, images_ref), (good_hbm, good_ref)]
    moves += list(zip(refs[:count], refs[count + 2 : -3]))
    copies = [
        pltpu.make_async_copy(source, target, semaphores.at[index])
        for index, (source, target) in enumerate(moves)
    ]
    for copy in copies:
        copy.start()
    copies[0].wait()
    copies[1].wait()
    weight = good_ref[...].astype(jnp.float32)
    weight_ref[...] = weight
    masked_ref[...] = images_ref[...].astype(jnp.float32) * weight
    for copy in copies[2:]:
        copy.wait()


def fit_kernel(
    select_ref,
    pair_ref,
    near_ref,
    far_ref,
    swapped_near_ref,
    swapped_far_ref,
    masked_ref,
    weight_ref,
    column_ref,
    row_ref,
    fold_ref,
    place_ref,
    coefs_ref,
    own_sum_ref,
    near_sum_ref,
    far_sum_ref,
    swap_sum_ref,
    window_ref,
    smooth_ref,
    basis_ref,
    parts_ref,
    sums_ref,
):
    epochs, rows, cols = masked_ref.shape
    blocks = cols // LANES
    groups = rows // SUB
    spreads = len(SIGMAS)
    kernels = spreads * DEGREES
    planes = NBASIS + 1
    height = planes * SUB
    f32, bf16 = jnp.float32, jnp.bfloat16

    sources = [pair_ref, near_ref, far_ref, swapped_near_ref, swapped_far_ref]
    lane = lax.broadcasted_iota(jnp.int32, (rows, cols + LANES), 1)
    inside = jnp.logical_and(lane >= KHALF, lane < cols + KHALF)
    for e in range(epochs):
        for index, source in enumerate(sources):

            @pl.when(select_ref[e] // 2 == index)
            def _():
                template = source[select_ref[e] % 2].astype(f32)
                wide = jnp.concatenate([template, template[:, :LANES]], 1)
                wide = jnp.where(inside, pltpu.roll(wide, KHALF, 1), 0.0).astype(bf16)
                for b in range(blocks):
                    at = (e * blocks + b) * rows
                    window_ref[at : at + rows, :] = wide[:, b * LANES : (b + 2) * LANES]

    sums_ref[...] = jnp.zeros_like(sums_ref)

    for k in range(0, kernels, 2):
        width = min(2, kernels - k)
        out = jnp.dot(
            window_ref[...],
            column_ref[:, k * LANES : (k + width) * LANES],
            preferred_element_type=f32,
        ).astype(bf16)
        for e in range(epochs):
            for b in range(blocks):
                at = (e * blocks + b) * rows
                for w in range(width):
                    to = (k + w) * cols + b * LANES
                    smooth_ref[e, :, to : to + LANES] = out[at : at + rows, w * LANES : (w + 1) * LANES]

    row_a = lax.broadcasted_iota(jnp.int32, (height, height), 0)
    row_b = lax.broadcasted_iota(jnp.int32, (height, height), 1)
    same_row = row_a % SUB == row_b % SUB
    wide = 2 * LANES
    for e in range(epochs):
        for at in range(0, cols, wide):
            held = {}

            def store(pair, first, second):
                for g in range(groups):
                    for h in range(0, wide, LANES):
                        mask = weight_ref[e, g * SUB : (g + 1) * SUB, at + h : at + h + LANES]
                        tiles = [first(g, h) * mask, second(g, h) * mask]
                        to = g * cols + at + h
                        basis_ref[e, 2 * pair * SUB : 2 * (pair + 1) * SUB, to : to + LANES] = (
                            jnp.concatenate(tiles, 0).astype(bf16)
                        )

            def degree(s, i, j):
                def tile(g, h):
                    row = (g * DEGREES + j) * SUB
                    return held[s, i][row : row + SUB, h : h + LANES]

                return tile

            for s in range(spreads):
                for i in range(DEGREES):
                    here = (s * DEGREES + i) * cols + at
                    held[s, i] = jnp.dot(
                        row_ref[s], smooth_ref[e, :, here : here + wide], preferred_element_type=f32
                    )
                    store(s * 4 + i, degree(s, i, 0), degree(s, i, 1))
                    if i == 1:
                        store(s * 4 + 3, degree(s, 0, 2), degree(s, 1, 2))
            store(12, degree(0, 2, 2), degree(1, 2, 2))
            store(
                13,
                degree(2, 2, 2),
                lambda g, h: masked_ref[e, g * SUB : (g + 1) * SUB, at + h : at + h + LANES],
            )
        basis = basis_ref[e]
        gram = lax.dot_general(
            basis, basis, (((1,), (1,)), ((), ())), preferred_element_type=f32
        )
        for index, part in enumerate(split3(jnp.where(same_row, gram, 0.0))):
            parts_ref[index, e] = part
    packed = jnp.zeros((height, LANES), f32)
    for index in range(3):
        for e in range(epochs):
            packed = packed + jnp.dot(
                parts_ref[index, e],
                place_ref[e * height : (e + 1) * height],
                preferred_element_type=f32,
            )
    system = jnp.zeros((SLOT, LANES), f32)
    for part in split3(packed):
        system = system + jnp.dot(fold_ref[...], part, preferred_element_type=f32)
    plane = lax.broadcasted_iota(jnp.int32, (SLOT, LANES), 0)
    lane = lax.broadcasted_iota(jnp.int32, (SLOT, LANES), 1)
    slot = lane % SLOT
    system = system / (rows * cols) + jnp.where(plane == slot, RIDGE_TERM, 0.0)
    start = lane - slot
    for p in range(0, NBASIS, 2):
        single = p == NBASIS - 1
        row_p = jnp.broadcast_to(system[p : p + 1], (SUB, LANES))
        near = start[:SUB] + p
        col_p = jnp.take_along_axis(system, start + p, axis=1)
        a = jnp.take_along_axis(row_p, near, axis=1)
        if single:
            u_p = jnp.concatenate([row_p / a] * (SLOT // SUB), 0)
            system = jnp.where(plane == p, u_p, system - col_p * u_p)
            continue
        row_q = jnp.broadcast_to(system[p + 1 : p + 2], (SUB, LANES))
        col_q = jnp.take_along_axis(system, start + (p + 1), axis=1)
        b = jnp.take_along_axis(row_p, near + 1, axis=1)
        d = jnp.take_along_axis(row_q, near + 1, axis=1)
        scale = 1.0 / (a * d - b * b)
        u_p = jnp.concatenate([(d * row_p - b * row_q) * scale] * (SLOT // SUB), 0)
        u_q = jnp.concatenate([(a * row_q - b * row_p) * scale] * (SLOT // SUB), 0)
        system = jnp.where(
            plane == p, u_p, jnp.where(plane == p + 1, u_q, system - col_p * u_p - col_q * u_q)
        )
    fold = fold_ref[...].astype(f32)
    sub = lax.broadcasted_iota(jnp.int32, (SUB, height), 0)
    of_row = lax.broadcasted_iota(jnp.int32, (SUB, height), 1) % SUB
    for e in range(epochs):
        at = e * SLOT + NBASIS
        column = jnp.broadcast_to(system[:, at : at + 1], (SLOT, LANES))
        coefs_ref[e : e + 1, :] = jnp.sum(jnp.where(plane == lane, column, 0.0), 0, keepdims=True)[
            :, :NBASIS
        ]
        column = jnp.where(plane < NBASIS, -column, jnp.where(plane == NBASIS, 1.0, 0.0))
        column = jnp.concatenate([column, column], 1)[:, :height]
        spread = jnp.sum(fold * column, 0, keepdims=True)
        left = jnp.where(sub == of_row, jnp.broadcast_to(spread, (SUB, height)), 0.0)
        high, middle, low = split3(left)
        left = jnp.concatenate([high, middle, low, jnp.zeros_like(low)], 0)
        target = select_ref[e]
        for g in range(groups):
            value = jnp.dot(
                left, basis_ref[e, :, g * cols : (g + 1) * cols], preferred_element_type=f32
            )
            here = (target, slice(g * SUB, (g + 1) * SUB))
            sums_ref[here] = sums_ref[here] + (
                value[:SUB] + (value[SUB : 2 * SUB] + value[2 * SUB : 3 * SUB])
            )
    own_sum_ref[...] = sums_ref[0:2]
    near_sum_ref[...] = sums_ref[2:4]
    far_sum_ref[...] = sums_ref[4:6]
    swap_sum_ref[...] = sums_ref[6:10].astype(bf16)


def between_cores(block):
    n = lax.axis_size(AXIS)
    return lax.ppermute(block, AXIS, [(i, i ^ 1) for i in range(n)])


def between_chips(block, distance):
    chips = lax.axis_size(AXIS) // CORES
    route = []
    for chip in range(chips):
        for core in range(CORES):
            origin = chip + (distance if core == 0 else -distance)
            if 0 <= origin < chips:
                route.append((CORES * origin + core, CORES * chip + core))
            else:
                route.append((CORES * chip + 1 - core, CORES * chip + core))
    return lax.ppermute(block, AXIS, route)


def buffer_of(epoch_patch):
    device = lax.axis_index(AXIS)
    core = device % CORES
    chip_offset = epoch_patch // CORES - device // CORES
    same_core = epoch_patch % CORES == core
    side = jnp.where(core == 0, 1, -1)
    far = jnp.abs(chip_offset) - 1
    mine = 2 + 2 * far + jnp.where(same_core, 0, 1)
    theirs = 6 + 2 * far + jnp.where(same_core, 1, 0)
    away = jnp.where(chip_offset * side > 0, mine, theirs)
    return jnp.where(chip_offset == 0, jnp.where(same_core, 0, 1), away).astype(jnp.int32)


def shards(templates, epoch_patch, images, good_pixels):
    epochs, rows, cols = images.shape
    f32, bf16 = jnp.float32, jnp.bfloat16
    assert templates.shape[0] == 1 and epochs * SLOT <= LANES
    assert lax.axis_size(AXIS) % CORES == 0 and cols % LANES == 0 and rows % SUB == 0
    other = between_cores(templates)
    pair = jnp.concatenate([templates, other], 0)
    near, far = between_chips(pair, 1), between_chips(pair, 2)
    swapped_near, swapped_far = between_cores(near), between_cores(far)
    taps = kernel_taps()
    height = (NBASIS + 1) * SUB
    tiles = epochs * (cols // LANES) * rows
    vmem, vmem_spec = pltpu.VMEM, pl.BlockSpec(memory_space=pltpu.VMEM)
    constants = (column_bands(taps), row_bands(taps, rows)) + plane_maps(epochs)
    sources = (images, good_pixels, *(jnp.asarray(c) for c in constants))
    prepared = pl.pallas_call(
        prepare_kernel,
        out_shape=[vmem((epochs, rows, cols), f32)] * 2 + [vmem(c.shape, bf16) for c in constants],
        in_specs=[pl.BlockSpec(memory_space=pltpu.HBM)] * (2 + len(constants)),
        out_specs=[vmem_spec] * (2 + len(constants)),
        scratch_shapes=[
            vmem(images.shape, bf16),
            vmem(good_pixels.shape, jnp.int32),
            pltpu.SemaphoreType.DMA((2 + len(constants),)),
        ],
        compiler_params=pltpu.CompilerParams(vmem_limit_bytes=4 << 20),
        name="prepare",
    )(*(pltpu.with_memory_space_constraint(x, pltpu.HBM) for x in sources))
    operands = (pair, near, far, swapped_near, swapped_far, *prepared)
    coefs, own_sum, near_sum, far_sum, swap_sum = pl.pallas_call(
        fit_kernel,
        out_shape=(
            jax.ShapeDtypeStruct((epochs, NBASIS), f32),
            vmem((2, rows, cols), f32),
            vmem((2, rows, cols), f32),
            vmem((2, rows, cols), f32),
            vmem((4, rows, cols), bf16),
        ),
        in_specs=[pl.BlockSpec(memory_space=pltpu.SMEM)] + [vmem_spec] * len(operands),
        out_specs=[vmem_spec] * 5,
        scratch_shapes=[
            vmem((tiles, 2 * LANES), bf16),
            vmem((epochs, rows, taps.shape[0] * cols), bf16),
            vmem((epochs, height, rows // SUB * cols), bf16),
            vmem((3, epochs, height, height), bf16),
            vmem((10, rows, cols), f32),
        ],
        compiler_params=pltpu.CompilerParams(vmem_limit_bytes=32 << 20),
        name="fit",
    )(
        buffer_of(epoch_patch),
        *(pltpu.with_memory_space_constraint(x, pltpu.VMEM) for x in operands),
    )
    received = between_cores(swap_sum)
    near_sum = (near_sum + received[0:2].astype(f32)).astype(bf16)
    far_sum = (far_sum + received[2:4].astype(f32)).astype(bf16)
    near_back, far_back = between_chips(near_sum, -1), between_chips(far_sum, -2)
    total = own_sum + near_back.astype(f32) + far_back.astype(f32)
    deep_sum = total[0:1] + between_cores(total[1:2].astype(bf16)).astype(f32)
    return (deep_sum, coefs)


def solution(mesh):
    spec = P(("tract", AXIS), None, None)
    in_specs = (spec, P(("tract", AXIS)), spec, spec)
    out_specs = (spec, P(("tract", AXIS), None))
    return jax.shard_map(shards, mesh=mesh, in_specs=in_specs, out_specs=out_specs, check_vma=False)
```

```python
from functools import partial

import jax
import jax.numpy as jnp
import numpy as np
from jax import lax
from jax.experimental import pallas as pl
from jax.experimental.pallas import tpu as pltpu
from jax.sharding import PartitionSpec as P

RADIUS = 4
KHALF = 9
SIGMAS = (1.0, 2.0, 4.0)
DEGREES = 3
NBASIS = (len(SIGMAS) * DEGREES) * DEGREES
RIDGE_TERM = 0.1
AXIS = "epoch"
CORES = 2
REACH = RADIUS // CORES
LANES = 128
SUB = 8
TAPS = 2 * KHALF + 1
SLOT = 32


def kernel_taps():
    places = np.arange(-KHALF, KHALF + 1).astype(np.float64)
    profiles = []
    for spread in SIGMAS:
        for degree in range(DEGREES):
            profile = places**degree * np.exp(-places * places / (2.0 * spread * spread))
            profiles.append(profile / np.sqrt(np.sum(profile * profile)))
    return np.stack(profiles).astype(np.float32).astype(jnp.bfloat16)


def column_bands(taps):
    kernels = taps.shape[0]
    bands = np.zeros((2 * LANES, kernels, LANES), taps.dtype)
    for x in range(LANES):
        for tap in range(TAPS):
            bands[x + 2 * KHALF - tap, :, x] = taps[:, tap]
    return bands.reshape(2 * LANES, kernels * LANES)


def row_bands(taps, rows):
    bands = np.zeros((len(SIGMAS), rows // SUB, DEGREES, SUB, rows), taps.dtype)
    for y in range(rows):
        for tap in range(TAPS):
            source = y - tap + KHALF
            if 0 <= source < rows:
                bands[:, y // SUB, :, y % SUB, source] = taps[:, tap].reshape(len(SIGMAS), DEGREES)
    return bands.reshape(len(SIGMAS), rows * DEGREES, rows)


def split3(x):
    high = x.astype(jnp.bfloat16)
    rest = x - high.astype(jnp.float32)
    middle = rest.astype(jnp.bfloat16)
    low = (rest - middle.astype(jnp.float32)).astype(jnp.bfloat16)
    return high, middle, low


def plane_order():
    order = []
    n = DEGREES
    for s in range(len(SIGMAS)):
        at = s * n * n
        for i in range(n):
            order += [at + i * n, at + i * n + 1]
        order += [at + 2, at + n + 2]
    order += [s * n * n + 2 * n + 2 for s in range(len(SIGMAS))]
    return order + [NBASIS]


def plane_maps(epochs):
    order = plane_order()
    height = len(order) * SUB
    fold = np.zeros((SLOT, height), np.float32)
    place = np.zeros((epochs, height, LANES), np.float32)
    for position, k in enumerate(order):
        rows = slice(position * SUB, (position + 1) * SUB)
        fold[k, rows] = 1
        for e in range(epochs):
            place[e, rows, e * SLOT + k] = 1
    return fold.astype(jnp.bfloat16), place.reshape(epochs * height, LANES).astype(jnp.bfloat16)


def prepare_kernel(images_hbm, good_hbm, *refs):
    count = (len(refs) - 5) // 2
    images_ref, good_ref, semaphores = refs[-3:]
    masked_ref, weight_ref = refs[count : count + 2]
    moves = [(images_hbm, images_ref), (good_hbm, good_ref)]
    moves += list(zip(refs[:count], refs[count + 2 : -3]))
    copies = [
        pltpu.make_async_copy(source, target, semaphores.at[index])
        for index, (source, target) in enumerate(moves)
    ]
    for copy in copies:
        copy.start()
    copies[0].wait()
    copies[1].wait()
    weight = good_ref[...].astype(jnp.float32)
    weight_ref[...] = weight
    masked_ref[...] = images_ref[...].astype(jnp.float32) * weight
    for copy in copies[2:]:
        copy.wait()


def fit_kernel(
    select_ref,
    pair_ref,
    near_ref,
    far_ref,
    swapped_near_ref,
    swapped_far_ref,
    masked_ref,
    weight_ref,
    column_ref,
    row_ref,
    fold_ref,
    place_ref,
    coefs_ref,
    own_sum_ref,
    near_sum_ref,
    far_sum_ref,
    swap_sum_ref,
    template_ref,
    window_ref,
    smooth_ref,
    basis_ref,
    parts_ref,
    sums_ref,
):
    epochs, rows, cols = masked_ref.shape
    blocks = cols // LANES
    groups = rows // SUB
    spreads = len(SIGMAS)
    kernels = spreads * DEGREES
    planes = NBASIS + 1
    height = planes * SUB
    f32, bf16 = jnp.float32, jnp.bfloat16

    sources = [pair_ref, near_ref, far_ref, swapped_near_ref, swapped_far_ref]
    for e in range(epochs):
        for index, source in enumerate(sources):

            @pl.when(select_ref[e] // 2 == index)
            def _():
                template_ref[e] = source[select_ref[e] % 2]

    lane = lax.broadcasted_iota(jnp.int32, (rows, cols + LANES), 1)
    inside = jnp.logical_and(lane >= KHALF, lane < cols + KHALF)
    for e in range(epochs):
        template = template_ref[e].astype(f32)
        wide = jnp.concatenate([template, template[:, :LANES]], 1)
        wide = jnp.where(inside, pltpu.roll(wide, KHALF, 1), 0.0).astype(bf16)
        for b in range(blocks):
            at = (e * blocks + b) * rows
            window_ref[at : at + rows, :] = wide[:, b * LANES : (b + 2) * LANES]

    sums_ref[...] = jnp.zeros_like(sums_ref)

    for k in range(0, kernels, 2):
        width = min(2, kernels - k)
        out = jnp.dot(
            window_ref[...],
            column_ref[:, k * LANES : (k + width) * LANES],
            preferred_element_type=f32,
        ).astype(bf16)
        for e in range(epochs):
            for b in range(blocks):
                at = (e * blocks + b) * rows
                for w in range(width):
                    to = (k + w) * cols + b * LANES
                    smooth_ref[e, :, to : to + LANES] = out[at : at + rows, w * LANES : (w + 1) * LANES]

    row_a = lax.broadcasted_iota(jnp.int32, (height, height), 0)
    row_b = lax.broadcasted_iota(jnp.int32, (height, height), 1)
    same_row = row_a % SUB == row_b % SUB
    wide = 2 * LANES
    systems = [jnp.zeros((SLOT, LANES), f32)] * epochs
    for e in range(epochs):
        for at in range(0, cols, wide):
            held = {}

            def store(pair, first, second):
                for g in range(groups):
                    for h in range(0, wide, LANES):
                        mask = weight_ref[e, g * SUB : (g + 1) * SUB, at + h : at + h + LANES]
                        tiles = [first(g, h) * mask, second(g, h) * mask]
                        to = g * cols + at + h
                        basis_ref[e, 2 * pair * SUB : 2 * (pair + 1) * SUB, to : to + LANES] = (
                            jnp.concatenate(tiles, 0).astype(bf16)
                        )

            def degree(s, i, j):
                def tile(g, h):
                    row = (g * DEGREES + j) * SUB
                    return held[s, i][row : row + SUB, h : h + LANES]

                return tile

            for s in range(spreads):
                for i in range(DEGREES):
                    here = (s * DEGREES + i) * cols + at
                    held[s, i] = jnp.dot(
                        row_ref[s], smooth_ref[e, :, here : here + wide], preferred_element_type=f32
                    )
                    store(s * 4 + i, degree(s, i, 0), degree(s, i, 1))
                    if i == 1:
                        store(s * 4 + 3, degree(s, 0, 2), degree(s, 1, 2))
            store(12, degree(0, 2, 2), degree(1, 2, 2))
            store(
                13,
                degree(2, 2, 2),
                lambda g, h: masked_ref[e, g * SUB : (g + 1) * SUB, at + h : at + h + LANES],
            )
        basis = basis_ref[e]
        gram = lax.dot_general(basis, basis, (((1,), (1,)), ((), ())), preferred_element_type=f32)
        for index, part in enumerate(split3(jnp.where(same_row, gram, 0.0))):
            parts_ref[index, e] = part
    packed = [jnp.zeros((height, LANES), f32)] * 2
    for index in range(3):
        for e in range(epochs):
            packed[e % 2] = packed[e % 2] + jnp.dot(
                parts_ref[index, e],
                place_ref[e * height : (e + 1) * height],
                preferred_element_type=f32,
            )
    system = jnp.zeros((SLOT, LANES), f32)
    for part in split3(packed[0] + packed[1]):
        system = system + jnp.dot(fold_ref[...], part, preferred_element_type=f32)
    plane = lax.broadcasted_iota(jnp.int32, (SLOT, LANES), 0)
    lane = lax.broadcasted_iota(jnp.int32, (SLOT, LANES), 1)
    slot = lane % SLOT
    system = system / (rows * cols) + jnp.where(plane == slot, RIDGE_TERM, 0.0)
    start = lane - slot
    column_of = [jnp.take_along_axis(system, start + l, axis=1) for l in range(NBASIS + 1)]
    direct, swapped = jnp.zeros((SLOT, LANES), f32), jnp.zeros((SLOT, LANES), f32)

    def line(l, p):
        return jnp.broadcast_to(column_of[l][p : p + 1], (SLOT, LANES))

    for p in range(0, NBASIS - 1, 2):
        q = p + 1
        a, b, d = line(p, p), line(q, p), line(q, q)
        scale = 1.0 / (a * d - b * b)
        a, b, d = a * scale, b * scale, d * scale
        outside = (plane != p) & (plane != q)
        from_p = jnp.where(outside, column_of[p] * d - column_of[q] * b, 0.0)
        from_q = jnp.where(outside, column_of[q] * a - column_of[p] * b, 0.0)
        direct = jnp.where(plane == p, d, jnp.where(plane == q, a, direct))
        swapped = jnp.where(outside, swapped, b)
        for l in range(p + 2, NBASIS + 1):
            column_of[l] = column_of[l] - from_p * line(l, p) - from_q * line(l, q)
    p = NBASIS - 1
    scale = 1.0 / line(p, p)
    direct = jnp.where(plane == p, scale, direct)
    right = column_of[NBASIS]
    right = right - jnp.where(plane != p, column_of[p] * scale, 0.0) * line(NBASIS, p)
    above, below = pltpu.roll(right, SLOT - 1, 0), pltpu.roll(right, 1, 0)
    solved = direct * right - swapped * jnp.where(plane % 2 == 0, above, below)
    fold = fold_ref[...].astype(f32)
    sub = lax.broadcasted_iota(jnp.int32, (SUB, height), 0)
    of_row = lax.broadcasted_iota(jnp.int32, (SUB, height), 1) % SUB
    for e in range(epochs):
        column = jnp.broadcast_to(solved[:, e * SLOT : e * SLOT + 1], (SLOT, LANES))
        coefs_ref[e : e + 1, :] = jnp.sum(jnp.where(plane == lane, column, 0.0), 0, keepdims=True)[
            :, :NBASIS
        ]
        column = jnp.where(plane < NBASIS, -column, jnp.where(plane == NBASIS, 1.0, 0.0))
        column = jnp.concatenate([column, column], 1)[:, :height]
        spread = jnp.sum(fold * column, 0, keepdims=True)
        left = jnp.where(sub == of_row, jnp.broadcast_to(spread, (SUB, height)), 0.0)
        high, middle, low = split3(left)
        left = jnp.concatenate([high, middle, low, jnp.zeros_like(low)], 0)
        target = select_ref[e]
        scale = [jnp.broadcast_to(column[k : k + 1, :LANES], (SUB, LANES)) for k in plane_order()]
        for g in range(groups // 2):
            value = jnp.dot(
                left, basis_ref[e, :, g * cols : (g + 1) * cols], preferred_element_type=f32
            )
            value = value[:SUB] + (value[SUB : 2 * SUB] + value[2 * SUB : 3 * SUB])
            here = (target, slice(g * SUB, (g + 1) * SUB))
            sums_ref[here] = sums_ref[here] + value
            g = g + groups // 2
            for b in range(blocks):
                to = g * cols + b * LANES
                tile = basis_ref[e, :, to : to + LANES].astype(f32)
                value = tile[NBASIS * SUB :]
                for k in range(NBASIS):
                    value = value + scale[k] * tile[k * SUB : (k + 1) * SUB]
                here = (target, slice(g * SUB, (g + 1) * SUB), slice(b * LANES, (b + 1) * LANES))
                sums_ref[here] = sums_ref[here] + value
    own_sum_ref[...] = sums_ref[0:2]
    near_sum_ref[...] = sums_ref[2:4]
    far_sum_ref[...] = sums_ref[4:6]
    swap_sum_ref[...] = sums_ref[6:10].astype(bf16)


def between_cores(block):
    n = lax.axis_size(AXIS)
    return lax.ppermute(block, AXIS, [(i, i ^ 1) for i in range(n)])


def between_chips(block, distance):
    chips = lax.axis_size(AXIS) // CORES
    route = []
    for chip in range(chips):
        for core in range(CORES):
            origin = chip + (distance if core == 0 else -distance)
            if 0 <= origin < chips:
                route.append((CORES * origin + core, CORES * chip + core))
            else:
                route.append((CORES * chip + 1 - core, CORES * chip + core))
    return lax.ppermute(block, AXIS, route)


def buffer_of(epoch_patch):
    device = lax.axis_index(AXIS)
    core = device % CORES
    chip_offset = epoch_patch // CORES - device // CORES
    same_core = epoch_patch % CORES == core
    side = jnp.where(core == 0, 1, -1)
    far = jnp.abs(chip_offset) - 1
    mine = 2 + 2 * far + jnp.where(same_core, 0, 1)
    theirs = 6 + 2 * far + jnp.where(same_core, 1, 0)
    away = jnp.where(chip_offset * side > 0, mine, theirs)
    return jnp.where(chip_offset == 0, jnp.where(same_core, 0, 1), away).astype(jnp.int32)


def shards(templates, epoch_patch, images, good_pixels):
    epochs, rows, cols = images.shape
    f32, bf16 = jnp.float32, jnp.bfloat16
    assert templates.shape[0] == 1 and epochs * SLOT <= LANES
    assert lax.axis_size(AXIS) % CORES == 0 and cols % LANES == 0 and rows % SUB == 0
    other = between_cores(templates)
    pair = jnp.concatenate([templates, other], 0)
    near, far = between_chips(pair, 1), between_chips(pair, 2)
    swapped_near, swapped_far = between_cores(near), between_cores(far)
    taps = kernel_taps()
    height = (NBASIS + 1) * SUB
    tiles = epochs * (cols // LANES) * rows
    vmem, vmem_spec = pltpu.VMEM, pl.BlockSpec(memory_space=pltpu.VMEM)
    constants = (column_bands(taps), row_bands(taps, rows)) + plane_maps(epochs)
    sources = (images, good_pixels, *(jnp.asarray(c) for c in constants))
    prepared = pl.pallas_call(
        prepare_kernel,
        out_shape=[vmem((epochs, rows, cols), f32)] * 2 + [vmem(c.shape, bf16) for c in constants],
        in_specs=[pl.BlockSpec(memory_space=pltpu.HBM)] * (2 + len(constants)),
        out_specs=[vmem_spec] * (2 + len(constants)),
        scratch_shapes=[
            vmem(images.shape, bf16),
            vmem(good_pixels.shape, jnp.int32),
            pltpu.SemaphoreType.DMA((2 + len(constants),)),
        ],
        compiler_params=pltpu.CompilerParams(vmem_limit_bytes=4 << 20),
        name="prepare",
    )(*(pltpu.with_memory_space_constraint(x, pltpu.HBM) for x in sources))
    operands = (pair, near, far, swapped_near, swapped_far, *prepared)
    coefs, own_sum, near_sum, far_sum, swap_sum = pl.pallas_call(
        fit_kernel,
        out_shape=(
            vmem((epochs, NBASIS), f32),
            vmem((2, rows, cols), f32),
            vmem((2, rows, cols), f32),
            vmem((2, rows, cols), f32),
            vmem((4, rows, cols), bf16),
        ),
        in_specs=[pl.BlockSpec(memory_space=pltpu.SMEM)] + [vmem_spec] * len(operands),
        out_specs=[vmem_spec] * 5,
        scratch_shapes=[
            vmem((epochs, rows, cols), bf16),
            vmem((tiles, 2 * LANES), bf16),
            vmem((epochs, rows, taps.shape[0] * cols), bf16),
            vmem((epochs, height, rows // SUB * cols), bf16),
            vmem((3, epochs, height, height), bf16),
            vmem((10, rows, cols), f32),
        ],
        compiler_params=pltpu.CompilerParams(vmem_limit_bytes=32 << 20),
        name="fit",
    )(
        buffer_of(epoch_patch),
        *(pltpu.with_memory_space_constraint(x, pltpu.VMEM) for x in operands),
    )
    received = between_cores(swap_sum)
    near_sum = (near_sum + received[0:2].astype(f32)).astype(bf16)
    far_sum = (far_sum + received[2:4].astype(f32)).astype(bf16)
    near_back, far_back = between_chips(near_sum, -1), between_chips(far_sum, -2)
    total = own_sum + near_back.astype(f32) + far_back.astype(f32)
    deep_sum = total[0:1] + between_cores(total[1:2].astype(bf16)).astype(f32)
    return (deep_sum, coefs)


def solution(mesh):
    spec = P(("tract", AXIS), None, None)
    in_specs = (spec, P(("tract", AXIS)), spec, spec)
    out_specs = (spec, P(("tract", AXIS), None))
    return jax.shard_map(shards, mesh=mesh, in_specs=in_specs, out_specs=out_specs, check_vma=False)
```

```python
from functools import partial

import jax
import jax.numpy as jnp
import numpy as np
from jax import lax
from jax.experimental import pallas as pl
from jax.experimental.pallas import tpu as pltpu
from jax.sharding import PartitionSpec as P

RADIUS = 4
KHALF = 9
SIGMAS = (1.0, 2.0, 4.0)
DEGREES = 3
NBASIS = (len(SIGMAS) * DEGREES) * DEGREES
RIDGE_TERM = 0.1
AXIS = "epoch"
CORES = 2
LANES = 128
SUB = 8
TAPS = 2 * KHALF + 1
SLOT = 32


def kernel_taps():
    places = np.arange(-KHALF, KHALF + 1).astype(np.float64)
    profiles = []
    for spread in SIGMAS:
        for degree in range(DEGREES):
            profile = places**degree * np.exp(-places * places / (2.0 * spread * spread))
            profiles.append(profile / np.sqrt(np.sum(profile * profile)))
    return np.stack(profiles).astype(np.float32).astype(jnp.bfloat16)


def column_bands(taps):
    kernels = taps.shape[0]
    bands = np.zeros((2 * LANES, kernels, LANES), taps.dtype)
    for x in range(LANES):
        for tap in range(TAPS):
            bands[x + 2 * KHALF - tap, :, x] = taps[:, tap]
    return bands.reshape(2 * LANES, kernels * LANES)


def row_bands(taps, rows):
    bands = np.zeros((len(SIGMAS), rows // SUB, DEGREES, SUB, rows), taps.dtype)
    for y in range(rows):
        for tap in range(TAPS):
            source = y - tap + KHALF
            if 0 <= source < rows:
                bands[:, y // SUB, :, y % SUB, source] = taps[:, tap].reshape(len(SIGMAS), DEGREES)
    return bands.reshape(len(SIGMAS), rows * DEGREES, rows)


def split3(x):
    high = x.astype(jnp.bfloat16)
    rest = x - high.astype(jnp.float32)
    middle = rest.astype(jnp.bfloat16)
    low = (rest - middle.astype(jnp.float32)).astype(jnp.bfloat16)
    return high, middle, low


def plane_order():
    order = []
    n = DEGREES
    for s in range(len(SIGMAS)):
        at = s * n * n
        for i in range(n):
            order += [at + i * n, at + i * n + 1]
        order += [at + 2, at + n + 2]
    order += [s * n * n + 2 * n + 2 for s in range(len(SIGMAS))]
    return order + [NBASIS]


def plane_maps(epochs):
    order = plane_order()
    height = len(order) * SUB
    fold = np.zeros((SLOT, height), np.float32)
    permute = np.zeros((SLOT, SLOT), np.float32)
    place = np.zeros((epochs, height, LANES), np.float32)
    for position, k in enumerate(order):
        rows = slice(position * SUB, (position + 1) * SUB)
        fold[k, rows] = 1
        permute[k, position] = 1
        for e in range(epochs):
            place[e, rows, e * SLOT + k] = 1
    return fold.astype(jnp.bfloat16), permute.astype(jnp.bfloat16), place.reshape(epochs * height, LANES).astype(jnp.bfloat16)


def prepare_kernel(images_hbm, good_hbm, *refs):
    count = (len(refs) - 5) // 2
    images_ref, good_ref, semaphores = refs[-3:]
    masked_ref, weight_ref = refs[count : count + 2]
    moves = [(images_hbm, images_ref), (good_hbm, good_ref)]
    moves += list(zip(refs[:count], refs[count + 2 : -3]))
    copies = [
        pltpu.make_async_copy(source, target, semaphores.at[index])
        for index, (source, target) in enumerate(moves)
    ]
    for copy in copies:
        copy.start()
    copies[0].wait()
    copies[1].wait()
    weight = good_ref[...].astype(jnp.float32)
    weight_ref[...] = weight
    masked_ref[...] = images_ref[...].astype(jnp.float32) * weight
    for copy in copies[2:]:
        copy.wait()


def fit_kernel(
    select_ref,
    pair_ref,
    near_ref,
    far_ref,
    swapped_near_ref,
    swapped_far_ref,
    masked_ref,
    weight_ref,
    column_ref,
    row_ref,
    fold_ref,
    permute_ref,
    place_ref,
    coefs_ref,
    own_sum_ref,
    near_sum_ref,
    far_sum_ref,
    swap_sum_ref,
    window_ref,
    smooth_ref,
    basis_ref,
    parts_ref,
    sums_ref,
):
    epochs, rows, cols = masked_ref.shape
    blocks = cols // LANES
    groups = rows // SUB
    spreads = len(SIGMAS)
    kernels = spreads * DEGREES
    planes = NBASIS + 1
    height = planes * SUB
    f32, bf16 = jnp.float32, jnp.bfloat16

    sources = [pair_ref, near_ref, far_ref, swapped_near_ref, swapped_far_ref]
    lane = lax.broadcasted_iota(jnp.int32, (rows, cols + LANES), 1)
    inside = jnp.logical_and(lane >= KHALF, lane < cols + KHALF)
    for e in range(epochs):
        kind, slot = select_ref[e] // 2, select_ref[e] % 2
        template = sources[0][slot]
        for index, source in enumerate(sources[1:], 1):
            template = jnp.where(kind == index, source[slot], template)
        template = template.astype(f32)
        wide = jnp.concatenate([template, template[:, :LANES]], 1)
        wide = jnp.where(inside, pltpu.roll(wide, KHALF, 1), 0.0).astype(bf16)
        for b in range(blocks):
            at = (e * blocks + b) * rows
            window_ref[at : at + rows, :] = wide[:, b * LANES : (b + 2) * LANES]

    sums_ref[...] = jnp.zeros_like(sums_ref)

    for k in range(0, kernels, 2):
        width = min(2, kernels - k)
        out = jnp.dot(
            window_ref[...],
            column_ref[:, k * LANES : (k + width) * LANES],
            preferred_element_type=f32,
        ).astype(bf16)
        for e in range(epochs):
            for b in range(blocks):
                at = (e * blocks + b) * rows
                for w in range(width):
                    to = (k + w) * cols + b * LANES
                    smooth_ref[e, :, to : to + LANES] = out[at : at + rows, w * LANES : (w + 1) * LANES]

    row_a = lax.broadcasted_iota(jnp.int32, (height, height), 0)
    row_b = lax.broadcasted_iota(jnp.int32, (height, height), 1)
    same_row = row_a % SUB == row_b % SUB
    wide = 2 * LANES
    systems = [jnp.zeros((SLOT, LANES), f32)] * epochs
    for e in range(epochs):
        for at in range(0, cols, wide):
            held = {}

            def store(pair, first, second):
                for g in range(groups):
                    for h in range(0, wide, LANES):
                        mask = weight_ref[e, g * SUB : (g + 1) * SUB, at + h : at + h + LANES]
                        tiles = [first(g, h) * mask, second(g, h) * mask]
                        to = g * cols + at + h
                        basis_ref[e, 2 * pair * SUB : 2 * (pair + 1) * SUB, to : to + LANES] = (
                            jnp.concatenate(tiles, 0).astype(bf16)
                        )

            def degree(s, i, j):
                def tile(g, h):
                    row = (g * DEGREES + j) * SUB
                    return held[s, i][row : row + SUB, h : h + LANES]

                return tile

            for s in range(spreads):
                for i in range(DEGREES):
                    here = (s * DEGREES + i) * cols + at
                    held[s, i] = jnp.dot(
                        row_ref[s], smooth_ref[e, :, here : here + wide], preferred_element_type=f32
                    )
                    store(s * 4 + i, degree(s, i, 0), degree(s, i, 1))
                    if i == 1:
                        store(s * 4 + 3, degree(s, 0, 2), degree(s, 1, 2))
            store(12, degree(0, 2, 2), degree(1, 2, 2))
            store(
                13,
                degree(2, 2, 2),
                lambda g, h: masked_ref[e, g * SUB : (g + 1) * SUB, at + h : at + h + LANES],
            )
        pieces = 2 if e == epochs - 1 else 1
        length = basis_ref.shape[2] // pieces
        gram = jnp.zeros((height, height), f32)
        for piece in range(pieces):
            basis = basis_ref[e, :, piece * length : (piece + 1) * length]
            product = lax.dot_general(
                basis, basis, (((1,), (1,)), ((), ())), preferred_element_type=f32
            )
            gram = gram + jnp.where(same_row, product, 0.0)
        gram = gram.reshape(planes, SUB, height).sum(1)
        gram = jnp.concatenate([gram, jnp.zeros((SLOT - planes, height), f32)], 0)
        for index, part in enumerate(split3(gram)):
            parts_ref[index, :, e * height : (e + 1) * height] = part
    system = jnp.zeros((SLOT, LANES), f32)
    for index in range(3):
        system = system + jnp.dot(parts_ref[index], place_ref[...], preferred_element_type=f32)
    system = sum(jnp.dot(permute_ref[...], part, preferred_element_type=f32) for part in split3(system))
    plane = lax.broadcasted_iota(jnp.int32, (SLOT, LANES), 0)
    lane = lax.broadcasted_iota(jnp.int32, (SLOT, LANES), 1)
    slot = lane % SLOT
    system = system / (rows * cols) + jnp.where(plane == slot, RIDGE_TERM, 0.0)
    start = lane - slot
    column_of = [jnp.take_along_axis(system, start + l, axis=1) for l in range(NBASIS + 1)]
    direct, swapped = jnp.zeros((SLOT, LANES), f32), jnp.zeros((SLOT, LANES), f32)

    def line(l, p):
        return jnp.broadcast_to(column_of[l][p : p + 1], (SLOT, LANES))

    for p in range(0, NBASIS - 1, 2):
        q = p + 1
        a, b, d = line(p, p), line(q, p), line(q, q)
        scale = 1.0 / (a * d - b * b)
        a, b, d = a * scale, b * scale, d * scale
        outside = (plane != p) & (plane != q)
        from_p = jnp.where(outside, column_of[p] * d - column_of[q] * b, 0.0)
        from_q = jnp.where(outside, column_of[q] * a - column_of[p] * b, 0.0)
        direct = jnp.where(plane == p, d, jnp.where(plane == q, a, direct))
        swapped = jnp.where(outside, swapped, b)
        for l in range(p + 2, NBASIS + 1):
            column_of[l] = column_of[l] - from_p * line(l, p) - from_q * line(l, q)
    p = NBASIS - 1
    scale = 1.0 / line(p, p)
    direct = jnp.where(plane == p, scale, direct)
    right = column_of[NBASIS]
    right = right - jnp.where(plane != p, column_of[p] * scale, 0.0) * line(NBASIS, p)
    above, below = pltpu.roll(right, SLOT - 1, 0), pltpu.roll(right, 1, 0)
    solved = direct * right - swapped * jnp.where(plane % 2 == 0, above, below)
    fold = fold_ref[...].astype(f32)
    sub = lax.broadcasted_iota(jnp.int32, (SUB, height), 0)
    of_row = lax.broadcasted_iota(jnp.int32, (SUB, height), 1) % SUB
    for e in range(epochs):
        column = jnp.broadcast_to(solved[:, e * SLOT : e * SLOT + 1], (SLOT, LANES))
        coefs_ref[e : e + 1, :] = jnp.sum(jnp.where(plane == lane, column, 0.0), 0, keepdims=True)[
            :, :NBASIS
        ]
        column = jnp.where(plane < NBASIS, -column, jnp.where(plane == NBASIS, 1.0, 0.0))
        column = jnp.concatenate([column, column], 1)[:, :height]
        spread = jnp.sum(fold * column, 0, keepdims=True)
        left = jnp.where(sub == of_row, jnp.broadcast_to(spread, (SUB, height)), 0.0)
        high, middle, low = split3(left)
        left = jnp.concatenate([high, middle, low, jnp.zeros_like(low)], 0)
        target = select_ref[e]
        scale = [jnp.broadcast_to(column[k : k + 1, :LANES], (SUB, LANES)) for k in plane_order()]
        for g in range(6):
            value = jnp.dot(
                left, basis_ref[e, :, g * cols : (g + 1) * cols], preferred_element_type=f32
            )
            value = value[:SUB] + (value[SUB : 2 * SUB] + value[2 * SUB : 3 * SUB])
            here = (target, slice(g * SUB, (g + 1) * SUB))
            sums_ref[here] = sums_ref[here] + value
        for g in range(6, groups):
            for b in range(blocks):
                to = g * cols + b * LANES
                tile = basis_ref[e, :, to : to + LANES].astype(f32)
                value = tile[NBASIS * SUB :]
                for k in range(NBASIS):
                    value = value + scale[k] * tile[k * SUB : (k + 1) * SUB]
                here = (target, slice(g * SUB, (g + 1) * SUB), slice(b * LANES, (b + 1) * LANES))
                sums_ref[here] = sums_ref[here] + value
    own_sum_ref[...] = sums_ref[0:2]
    near_sum_ref[...] = sums_ref[2:4]
    far_sum_ref[...] = sums_ref[4:6]
    swap_sum_ref[...] = sums_ref[6:10].astype(bf16)


def between_cores(block):
    n = lax.axis_size(AXIS)
    return lax.ppermute(block, AXIS, [(i, i ^ 1) for i in range(n)])


def between_chips(block, distance):
    chips = lax.axis_size(AXIS) // CORES
    route = []
    for chip in range(chips):
        for core in range(CORES):
            origin = chip + (distance if core == 0 else -distance)
            if 0 <= origin < chips:
                route.append((CORES * origin + core, CORES * chip + core))
            else:
                route.append((CORES * chip + 1 - core, CORES * chip + core))
    return lax.ppermute(block, AXIS, route)


def buffer_of(epoch_patch):
    device = lax.axis_index(AXIS)
    core = device % CORES
    chip_offset = epoch_patch // CORES - device // CORES
    same_core = epoch_patch % CORES == core
    side = jnp.where(core == 0, 1, -1)
    far = jnp.abs(chip_offset) - 1
    mine = 2 + 2 * far + jnp.where(same_core, 0, 1)
    theirs = 6 + 2 * far + jnp.where(same_core, 1, 0)
    away = jnp.where(chip_offset * side > 0, mine, theirs)
    return jnp.where(chip_offset == 0, jnp.where(same_core, 0, 1), away).astype(jnp.int32)


def shards(templates, epoch_patch, images, good_pixels):
    epochs, rows, cols = images.shape
    f32, bf16 = jnp.float32, jnp.bfloat16
    assert templates.shape[0] == 1 and epochs * SLOT <= LANES
    assert lax.axis_size(AXIS) % CORES == 0 and cols % LANES == 0 and rows % SUB == 0
    other = between_cores(templates)
    pair = jnp.concatenate([templates, other], 0)
    near, far = between_chips(pair, 1), between_chips(pair, 2)
    swapped_near, swapped_far = between_cores(near), between_cores(far)
    taps = kernel_taps()
    height = (NBASIS + 1) * SUB
    tiles = epochs * (cols // LANES) * rows
    vmem, vmem_spec = pltpu.VMEM, pl.BlockSpec(memory_space=pltpu.VMEM)
    constants = (column_bands(taps), row_bands(taps, rows)) + plane_maps(epochs)
    sources = (images, good_pixels, *(jnp.asarray(c) for c in constants))
    prepared = pl.pallas_call(
        prepare_kernel,
        out_shape=[vmem((epochs, rows, cols), f32)] * 2 + [vmem(c.shape, bf16) for c in constants],
        in_specs=[pl.BlockSpec(memory_space=pltpu.HBM)] * (2 + len(constants)),
        out_specs=[vmem_spec] * (2 + len(constants)),
        scratch_shapes=[
            vmem(images.shape, bf16),
            vmem(good_pixels.shape, jnp.int32),
            pltpu.SemaphoreType.DMA((2 + len(constants),)),
        ],
        compiler_params=pltpu.CompilerParams(vmem_limit_bytes=4 << 20),
        name="prepare",
    )(*(pltpu.with_memory_space_constraint(x, pltpu.HBM) for x in sources))
    operands = (pair, near, far, swapped_near, swapped_far, *prepared)
    coefs, own_sum, near_sum, far_sum, swap_sum = pl.pallas_call(
        fit_kernel,
        out_shape=(
            vmem((epochs, NBASIS), f32),
            vmem((2, rows, cols), f32),
            vmem((2, rows, cols), f32),
            vmem((2, rows, cols), f32),
            vmem((4, rows, cols), bf16),
        ),
        in_specs=[pl.BlockSpec(memory_space=pltpu.SMEM)] + [vmem_spec] * len(operands),
        out_specs=[vmem_spec] * 5,
        scratch_shapes=[
            vmem((tiles, 2 * LANES), bf16),
            vmem((epochs, rows, taps.shape[0] * cols), bf16),
            vmem((epochs, height, rows // SUB * cols), bf16),
            vmem((3, SLOT, epochs * height), bf16),
            vmem((10, rows, cols), f32),
        ],
        compiler_params=pltpu.CompilerParams(vmem_limit_bytes=32 << 20),
        name="fit",
    )(
        buffer_of(epoch_patch),
        *(pltpu.with_memory_space_constraint(x, pltpu.VMEM) for x in operands),
    )
    received = between_cores(swap_sum)
    near_sum = (near_sum + received[0:2].astype(f32)).astype(bf16)
    far_sum = (far_sum + received[2:4].astype(f32)).astype(bf16)
    near_back, far_back = between_chips(near_sum, -1), between_chips(far_sum, -2)
    total = own_sum + near_back.astype(f32) + far_back.astype(f32)
    deep_sum = total[0:1] + between_cores(total[1:2].astype(bf16)).astype(f32)
    return (deep_sum, coefs)


def solution(mesh):
    spec = P(("tract", AXIS), None, None)
    in_specs = (spec, P(("tract", AXIS)), spec, spec)
    out_specs = (spec, P(("tract", AXIS), None))
    return jax.shard_map(shards, mesh=mesh, in_specs=in_specs, out_specs=out_specs, check_vma=False)
```

```python
from functools import partial

import jax
import jax.numpy as jnp
import numpy as np
from jax import lax
from jax.experimental import pallas as pl
from jax.experimental.pallas import tpu as pltpu
from jax.sharding import PartitionSpec as P

RADIUS = 4
KHALF = 9
SIGMAS = (1.0, 2.0, 4.0)
DEGREES = 3
NBASIS = (len(SIGMAS) * DEGREES) * DEGREES
RIDGE_TERM = 0.1
AXIS = "epoch"
CORES = 2
LANES = 128
SUB = 8
TAPS = 2 * KHALF + 1
SLOT = 32


def kernel_taps():
    places = np.arange(-KHALF, KHALF + 1).astype(np.float64)
    profiles = []
    for spread in SIGMAS:
        for degree in range(DEGREES):
            profile = places**degree * np.exp(-places * places / (2.0 * spread * spread))
            profiles.append(profile / np.sqrt(np.sum(profile * profile)))
    return np.stack(profiles).astype(np.float32).astype(jnp.bfloat16)


def column_bands(taps):
    kernels = taps.shape[0]
    bands = np.zeros((2 * LANES, kernels, LANES), taps.dtype)
    for x in range(LANES):
        for tap in range(TAPS):
            bands[x + 2 * KHALF - tap, :, x] = taps[:, tap]
    return bands.reshape(2 * LANES, kernels * LANES)


def row_bands(taps, rows):
    bands = np.zeros((len(SIGMAS), rows // SUB, DEGREES, SUB, rows), taps.dtype)
    for y in range(rows):
        for tap in range(TAPS):
            source = y - tap + KHALF
            if 0 <= source < rows:
                bands[:, y // SUB, :, y % SUB, source] = taps[:, tap].reshape(len(SIGMAS), DEGREES)
    return bands.reshape(len(SIGMAS), rows * DEGREES, rows)


def split3(x):
    high = x.astype(jnp.bfloat16)
    rest = x - high.astype(jnp.float32)
    middle = rest.astype(jnp.bfloat16)
    low = (rest - middle.astype(jnp.float32)).astype(jnp.bfloat16)
    return high, middle, low


def plane_order():
    order = []
    n = DEGREES
    for s in range(len(SIGMAS)):
        at = s * n * n
        for i in range(n):
            order += [at + i * n, at + i * n + 1]
        order += [at + 2, at + n + 2]
    order += [s * n * n + 2 * n + 2 for s in range(len(SIGMAS))]
    return order + [NBASIS]


def plane_maps(epochs):
    order = plane_order()
    height = len(order) * SUB
    natural = np.zeros((SLOT, SLOT), np.float32)
    place = np.zeros((epochs, height, LANES), np.float32)
    for position, k in enumerate(order):
        natural[position, k] = 1
        for e in range(epochs):
            place[e, position * SUB : (position + 1) * SUB, e * SLOT + position] = 1
    return natural.astype(jnp.bfloat16), place.reshape(epochs * height, LANES).astype(jnp.bfloat16)


def prepare_kernel(images_hbm, good_hbm, *refs):
    count = (len(refs) - 5) // 2
    images_ref, good_ref, semaphores = refs[-3:]
    masked_ref, weight_ref = refs[count : count + 2]
    moves = [(images_hbm, images_ref), (good_hbm, good_ref)]
    moves += list(zip(refs[:count], refs[count + 2 : -3]))
    copies = [
        pltpu.make_async_copy(source, target, semaphores.at[index])
        for index, (source, target) in enumerate(moves)
    ]
    for copy in copies:
        copy.start()
    copies[0].wait()
    copies[1].wait()
    weight = good_ref[...].astype(jnp.float32)
    weight_ref[...] = weight
    masked_ref[...] = images_ref[...].astype(jnp.float32) * weight
    for copy in copies[2:]:
        copy.wait()


def fit_kernel(
    select_ref,
    pair_ref,
    near_ref,
    far_ref,
    swapped_near_ref,
    swapped_far_ref,
    masked_ref,
    weight_ref,
    column_ref,
    row_ref,
    natural_ref,
    place_ref,
    coefs_ref,
    sums_ref,
    swap_sum_ref,
    window_ref,
    smooth_ref,
    basis_ref,
    parts_ref,
):
    epochs, rows, cols = masked_ref.shape
    blocks = cols // LANES
    groups = rows // SUB
    spreads = len(SIGMAS)
    kernels = spreads * DEGREES
    planes = NBASIS + 1
    height = planes * SUB
    f32, bf16 = jnp.float32, jnp.bfloat16

    sources = [pair_ref, near_ref, far_ref, swapped_near_ref, swapped_far_ref]
    lane = lax.broadcasted_iota(jnp.int32, (rows, cols + LANES), 1)
    inside = jnp.logical_and(lane >= KHALF, lane < cols + KHALF)
    for e in range(epochs):
        kind, slot = select_ref[e] // 2, select_ref[e] % 2
        template = sources[0][slot]
        for index, source in enumerate(sources[1:], 1):
            template = jnp.where(kind == index, source[slot], template)
        template = template.astype(f32)
        wide = jnp.concatenate([template, template[:, :LANES]], 1)
        wide = jnp.where(inside, pltpu.roll(wide, KHALF, 1), 0.0).astype(bf16)
        for b in range(blocks):
            at = (e * blocks + b) * rows
            window_ref[at : at + rows, :] = wide[:, b * LANES : (b + 2) * LANES]

    sums_ref[...] = jnp.zeros_like(sums_ref)

    for k in range(0, kernels, 2):
        width = min(2, kernels - k)
        out = jnp.dot(
            window_ref[...],
            column_ref[:, k * LANES : (k + width) * LANES],
            preferred_element_type=f32,
        ).astype(bf16)
        for e in range(epochs):
            for b in range(blocks):
                at = (e * blocks + b) * rows
                for w in range(width):
                    to = (k + w) * cols + b * LANES
                    smooth_ref[e, :, to : to + LANES] = out[at : at + rows, w * LANES : (w + 1) * LANES]

    row_a = lax.broadcasted_iota(jnp.int32, (height, height), 0)
    row_b = lax.broadcasted_iota(jnp.int32, (height, height), 1)
    same_row = row_a % SUB == row_b % SUB
    wide = 2 * LANES
    systems = [jnp.zeros((SLOT, LANES), f32)] * epochs
    for e in range(epochs):
        for at in range(0, cols, wide):
            held = {}

            def store(pair, first, second):
                for g in range(groups):
                    for h in range(0, wide, LANES):
                        mask = weight_ref[e, g * SUB : (g + 1) * SUB, at + h : at + h + LANES]
                        tiles = [first(g, h) * mask, second(g, h) * mask]
                        to = g * cols + at + h
                        basis_ref[e, 2 * pair * SUB : 2 * (pair + 1) * SUB, to : to + LANES] = (
                            jnp.concatenate(tiles, 0).astype(bf16)
                        )

            def degree(s, i, j):
                def tile(g, h):
                    row = (g * DEGREES + j) * SUB
                    return held[s, i][row : row + SUB, h : h + LANES]

                return tile

            for s in range(spreads):
                for i in range(DEGREES):
                    here = (s * DEGREES + i) * cols + at
                    held[s, i] = jnp.dot(
                        row_ref[s], smooth_ref[e, :, here : here + wide], preferred_element_type=f32
                    )
                    store(s * 4 + i, degree(s, i, 0), degree(s, i, 1))
                    if i == 1:
                        store(s * 4 + 3, degree(s, 0, 2), degree(s, 1, 2))
            store(12, degree(0, 2, 2), degree(1, 2, 2))
            store(
                13,
                degree(2, 2, 2),
                lambda g, h: masked_ref[e, g * SUB : (g + 1) * SUB, at + h : at + h + LANES],
            )
        pieces = 2 if e == epochs - 1 else 1
        length = basis_ref.shape[2] // pieces
        gram = jnp.zeros((height, height), f32)
        for piece in range(pieces):
            basis = basis_ref[e, :, piece * length : (piece + 1) * length]
            product = lax.dot_general(
                basis, basis, (((1,), (1,)), ((), ())), preferred_element_type=f32
            )
            gram = gram + jnp.where(same_row, product, 0.0)
        gram = gram.reshape(planes, SUB, height).sum(1)
        gram = jnp.concatenate([gram, jnp.zeros((SLOT - planes, height), f32)], 0)
        for index, part in enumerate(split3(gram)):
            parts_ref[index, :, e * height : (e + 1) * height] = part
    system = jnp.zeros((SLOT, LANES), f32)
    for index in range(3):
        system = system + jnp.dot(parts_ref[index], place_ref[...], preferred_element_type=f32)
    plane = lax.broadcasted_iota(jnp.int32, (SLOT, LANES), 0)
    lane = lax.broadcasted_iota(jnp.int32, (SLOT, LANES), 1)
    slot = lane % SLOT
    system = system / (rows * cols) + jnp.where(plane == slot, RIDGE_TERM, 0.0)
    start = lane - slot
    column_of = [jnp.take_along_axis(system, start + l, axis=1) for l in range(NBASIS + 1)]
    direct, swapped = jnp.zeros((SLOT, LANES), f32), jnp.zeros((SLOT, LANES), f32)

    def line(l, p):
        return jnp.broadcast_to(column_of[l][p : p + 1], (SLOT, LANES))

    for p in range(0, NBASIS - 1, 2):
        q = p + 1
        a, b, d = line(p, p), line(q, p), line(q, q)
        scale = 1.0 / (a * d - b * b)
        a, b, d = a * scale, b * scale, d * scale
        outside = (plane != p) & (plane != q)
        from_p = jnp.where(outside, column_of[p] * d - column_of[q] * b, 0.0)
        from_q = jnp.where(outside, column_of[q] * a - column_of[p] * b, 0.0)
        direct = jnp.where(plane == p, d, jnp.where(plane == q, a, direct))
        swapped = jnp.where(outside, swapped, b)
        for l in range(p + 2, NBASIS + 1):
            column_of[l] = column_of[l] - from_p * line(l, p) - from_q * line(l, q)
    p = NBASIS - 1
    scale = 1.0 / line(p, p)
    direct = jnp.where(plane == p, scale, direct)
    right = column_of[NBASIS]
    right = right - jnp.where(plane != p, column_of[p] * scale, 0.0) * line(NBASIS, p)
    above, below = pltpu.roll(right, SLOT - 1, 0), pltpu.roll(right, 1, 0)
    solved = direct * right - swapped * jnp.where(plane % 2 == 0, above, below)
    natural = natural_ref[...].astype(f32)
    fold = (
        lax.broadcasted_iota(jnp.int32, (SLOT, height), 0)
        == lax.broadcasted_iota(jnp.int32, (SLOT, height), 1) // SUB
    ).astype(f32)
    sub = lax.broadcasted_iota(jnp.int32, (SUB, height), 0)
    of_row = lax.broadcasted_iota(jnp.int32, (SUB, height), 1) % SUB
    for e in range(epochs):
        column = jnp.broadcast_to(solved[:, e * SLOT : e * SLOT + 1], (SLOT, LANES))
        coefs_ref[e : e + 1, :] = jnp.sum(natural * column[:, :SLOT], 0, keepdims=True)[:, :NBASIS]
        column = jnp.where(plane < NBASIS, -column, jnp.where(plane == NBASIS, 1.0, 0.0))
        column = jnp.concatenate([column, column], 1)[:, :height]
        spread = jnp.sum(fold * column, 0, keepdims=True)
        left = jnp.where(sub == of_row, jnp.broadcast_to(spread, (SUB, height)), 0.0)
        high, middle, low = split3(left)
        left = jnp.concatenate([high, middle, low, jnp.zeros_like(low)], 0)
        target = select_ref[e]
        scale = [jnp.broadcast_to(column[k : k + 1, :LANES], (SUB, LANES)) for k in range(NBASIS)]
        for g in range(6):
            value = jnp.dot(
                left, basis_ref[e, :, g * cols : (g + 1) * cols], preferred_element_type=f32
            )
            value = value[:SUB] + (value[SUB : 2 * SUB] + value[2 * SUB : 3 * SUB])
            here = (target, slice(g * SUB, (g + 1) * SUB))
            sums_ref[here] = sums_ref[here] + value
        for g in range(6, groups):
            for b in range(blocks):
                to = g * cols + b * LANES
                tile = basis_ref[e, :, to : to + LANES].astype(f32)
                value = tile[NBASIS * SUB :]
                for k in range(NBASIS):
                    value = value + scale[k] * tile[k * SUB : (k + 1) * SUB]
                here = (target, slice(g * SUB, (g + 1) * SUB), slice(b * LANES, (b + 1) * LANES))
                sums_ref[here] = sums_ref[here] + value
    swap_sum_ref[...] = sums_ref[6:10].astype(bf16)


def between_cores(block):
    n = lax.axis_size(AXIS)
    return lax.ppermute(block, AXIS, [(i, i ^ 1) for i in range(n)])


def between_chips(block, distance):
    chips = lax.axis_size(AXIS) // CORES
    route = []
    for chip in range(chips):
        for core in range(CORES):
            origin = chip + (distance if core == 0 else -distance)
            if 0 <= origin < chips:
                route.append((CORES * origin + core, CORES * chip + core))
            else:
                route.append((CORES * chip + 1 - core, CORES * chip + core))
    return lax.ppermute(block, AXIS, route)


def buffer_of(epoch_patch):
    device = lax.axis_index(AXIS)
    core = device % CORES
    chip_offset = epoch_patch // CORES - device // CORES
    same_core = epoch_patch % CORES == core
    side = jnp.where(core == 0, 1, -1)
    far = jnp.abs(chip_offset) - 1
    mine = 2 + 2 * far + jnp.where(same_core, 0, 1)
    theirs = 6 + 2 * far + jnp.where(same_core, 1, 0)
    away = jnp.where(chip_offset * side > 0, mine, theirs)
    return jnp.where(chip_offset == 0, jnp.where(same_core, 0, 1), away).astype(jnp.int32)


def shards(templates, epoch_patch, images, good_pixels):
    epochs, rows, cols = images.shape
    f32, bf16 = jnp.float32, jnp.bfloat16
    assert templates.shape[0] == 1 and epochs * SLOT <= LANES
    assert lax.axis_size(AXIS) % CORES == 0 and cols % LANES == 0 and rows % SUB == 0
    other = between_cores(templates)
    pair = jnp.concatenate([templates, other], 0)
    near, far = between_chips(pair, 1), between_chips(pair, 2)
    swapped_near, swapped_far = between_cores(near), between_cores(far)
    taps = kernel_taps()
    height = (NBASIS + 1) * SUB
    tiles = epochs * (cols // LANES) * rows
    vmem, vmem_spec = pltpu.VMEM, pl.BlockSpec(memory_space=pltpu.VMEM)
    constants = (column_bands(taps), row_bands(taps, rows)) + plane_maps(epochs)
    sources = (images, good_pixels, *(jnp.asarray(c) for c in constants))
    prepared = pl.pallas_call(
        prepare_kernel,
        out_shape=[vmem((epochs, rows, cols), f32)] * 2 + [vmem(c.shape, bf16) for c in constants],
        in_specs=[pl.BlockSpec(memory_space=pltpu.HBM)] * (2 + len(constants)),
        out_specs=[vmem_spec] * (2 + len(constants)),
        scratch_shapes=[
            vmem(images.shape, bf16),
            vmem(good_pixels.shape, jnp.int32),
            pltpu.SemaphoreType.DMA((2 + len(constants),)),
        ],
        compiler_params=pltpu.CompilerParams(vmem_limit_bytes=4 << 20),
        name="prepare",
    )(*(pltpu.with_memory_space_constraint(x, pltpu.HBM) for x in sources))
    operands = (pair, near, far, swapped_near, swapped_far, *prepared)
    coefs, sums, swap_sum = pl.pallas_call(
        fit_kernel,
        out_shape=(
            vmem((epochs, NBASIS), f32),
            vmem((10, rows, cols), f32),
            vmem((4, rows, cols), bf16),
        ),
        in_specs=[pl.BlockSpec(memory_space=pltpu.SMEM)] + [vmem_spec] * len(operands),
        out_specs=[vmem_spec] * 3,
        scratch_shapes=[
            vmem((tiles, 2 * LANES), bf16),
            vmem((epochs, rows, taps.shape[0] * cols), bf16),
            vmem((epochs, height, rows // SUB * cols), bf16),
            vmem((3, SLOT, epochs * height), bf16),
        ],
        compiler_params=pltpu.CompilerParams(vmem_limit_bytes=32 << 20),
        name="fit",
    )(
        buffer_of(epoch_patch),
        *(pltpu.with_memory_space_constraint(x, pltpu.VMEM) for x in operands),
    )
    received = between_cores(swap_sum)
    near_sum = (sums[2:4] + received[0:2].astype(f32)).astype(bf16)
    far_sum = (sums[4:6] + received[2:4].astype(f32)).astype(bf16)
    near_back, far_back = between_chips(near_sum, -1), between_chips(far_sum, -2)
    total = sums[0:2] + near_back.astype(f32) + far_back.astype(f32)
    deep_sum = total[0:1] + between_cores(total[1:2].astype(bf16)).astype(f32)
    return (deep_sum, coefs)


def solution(mesh):
    spec = P(("tract", AXIS), None, None)
    in_specs = (spec, P(("tract", AXIS)), spec, spec)
    out_specs = (spec, P(("tract", AXIS), None))
    return jax.shard_map(shards, mesh=mesh, in_specs=in_specs, out_specs=out_specs, check_vma=False)
```

```python
from functools import partial

import jax
import jax.numpy as jnp
import numpy as np
from jax import lax
from jax.experimental import pallas as pl
from jax.experimental.pallas import tpu as pltpu
from jax.sharding import PartitionSpec as P

RADIUS = 4
KHALF = 9
SIGMAS = (1.0, 2.0, 4.0)
DEGREES = 3
NBASIS = (len(SIGMAS) * DEGREES) * DEGREES
RIDGE_TERM = 0.1
AXIS = "epoch"
CORES = 2
LANES = 128
SUB = 8
TAPS = 2 * KHALF + 1
SLOT = 32


def kernel_taps():
    places = np.arange(-KHALF, KHALF + 1).astype(np.float64)
    profiles = []
    for spread in SIGMAS:
        for degree in range(DEGREES):
            profile = places**degree * np.exp(-places * places / (2.0 * spread * spread))
            profiles.append(profile / np.sqrt(np.sum(profile * profile)))
    return np.stack(profiles).astype(np.float32).astype(jnp.bfloat16)


def column_bands(taps):
    kernels = taps.shape[0]
    bands = np.zeros((2 * LANES, kernels, LANES), taps.dtype)
    for x in range(LANES):
        for tap in range(TAPS):
            bands[x + 2 * KHALF - tap, :, x] = taps[:, tap]
    return bands.reshape(2 * LANES, kernels * LANES)


def row_bands(taps, rows):
    bands = np.zeros((len(SIGMAS), rows // SUB, DEGREES, SUB, rows), taps.dtype)
    for y in range(rows):
        for tap in range(TAPS):
            source = y - tap + KHALF
            if 0 <= source < rows:
                bands[:, y // SUB, :, y % SUB, source] = taps[:, tap].reshape(len(SIGMAS), DEGREES)
    return bands.reshape(len(SIGMAS), rows * DEGREES, rows)


def split3(x):
    high = x.astype(jnp.bfloat16)
    rest = x - high.astype(jnp.float32)
    middle = rest.astype(jnp.bfloat16)
    low = (rest - middle.astype(jnp.float32)).astype(jnp.bfloat16)
    return high, middle, low


def plane_order():
    order = []
    n = DEGREES
    for s in range(len(SIGMAS)):
        at = s * n * n
        for i in range(n):
            order += [at + i * n, at + i * n + 1]
        order += [at + 2, at + n + 2]
    order += [s * n * n + 2 * n + 2 for s in range(len(SIGMAS))]
    return order + [NBASIS]


def plane_maps(epochs):
    order = plane_order()
    height = len(order) * SUB
    natural = np.zeros((SLOT, SLOT), np.float32)
    place = np.zeros((epochs, height, LANES), np.float32)
    for position, k in enumerate(order):
        natural[position, k] = 1
        for e in range(epochs):
            place[e, position * SUB : (position + 1) * SUB, e * SLOT + position] = 1
    return natural.astype(jnp.bfloat16), place.reshape(epochs * height, LANES).astype(jnp.bfloat16)


def prepare_kernel(images_hbm, good_hbm, *refs):
    count = (len(refs) - 5) // 2
    images_ref, good_ref, semaphores = refs[-3:]
    masked_ref, weight_ref = refs[count : count + 2]
    moves = [(images_hbm, images_ref), (good_hbm, good_ref)]
    moves += list(zip(refs[:count], refs[count + 2 : -3]))
    copies = [
        pltpu.make_async_copy(source, target, semaphores.at[index])
        for index, (source, target) in enumerate(moves)
    ]
    for copy in copies:
        copy.start()
    copies[0].wait()
    copies[1].wait()
    weight = good_ref[...].astype(jnp.float32)
    weight_ref[...] = weight
    masked_ref[...] = images_ref[...].astype(jnp.float32) * weight
    for copy in copies[2:]:
        copy.wait()


def fit_kernel(
    select_ref,
    pair_ref,
    near_ref,
    far_ref,
    swapped_near_ref,
    swapped_far_ref,
    masked_ref,
    weight_ref,
    column_ref,
    row_ref,
    natural_ref,
    place_ref,
    coefs_ref,
    sums_ref,
    swap_sum_ref,
    window_ref,
    smooth_ref,
    basis_ref,
    parts_ref,
):
    epochs, rows, cols = masked_ref.shape
    blocks = cols // LANES
    groups = rows // SUB
    spreads = len(SIGMAS)
    kernels = spreads * DEGREES
    planes = NBASIS + 1
    height = planes * SUB
    f32, bf16 = jnp.float32, jnp.bfloat16

    sources = [pair_ref, near_ref, far_ref, swapped_near_ref, swapped_far_ref]
    lane = lax.broadcasted_iota(jnp.int32, (rows, cols + LANES), 1)
    inside = jnp.logical_and(lane >= KHALF, lane < cols + KHALF)
    for e in range(epochs):
        kind, slot = select_ref[e] // 2, select_ref[e] % 2
        template = sources[0][slot]
        for index, source in enumerate(sources[1:], 1):
            template = jnp.where(kind == index, source[slot], template)
        template = template.astype(f32)
        wide = jnp.concatenate([template, template[:, :LANES]], 1)
        wide = jnp.where(inside, pltpu.roll(wide, KHALF, 1), 0.0).astype(bf16)
        for b in range(blocks):
            at = (e * blocks + b) * rows
            window_ref[at : at + rows, :] = wide[:, b * LANES : (b + 2) * LANES]

    sums_ref[...] = jnp.zeros_like(sums_ref)

    for k in range(0, kernels, 2):
        width = min(2, kernels - k)
        out = jnp.dot(
            window_ref[...],
            column_ref[:, k * LANES : (k + width) * LANES],
            preferred_element_type=f32,
        ).astype(bf16)
        for e in range(epochs):
            for b in range(blocks):
                at = (e * blocks + b) * rows
                for w in range(width):
                    to = (k + w) * cols + b * LANES
                    smooth_ref[e, :, to : to + LANES] = out[at : at + rows, w * LANES : (w + 1) * LANES]

    row_a = lax.broadcasted_iota(jnp.int32, (height, height), 0)
    row_b = lax.broadcasted_iota(jnp.int32, (height, height), 1)
    same_row = row_a % SUB == row_b % SUB
    wide = 2 * LANES
    systems = [jnp.zeros((SLOT, LANES), f32)] * epochs
    for e in range(epochs):
        for at in range(0, cols, wide):
            held = {}

            def store(pair, first, second):
                for g in range(groups):
                    for h in range(0, wide, LANES):
                        mask = weight_ref[e, g * SUB : (g + 1) * SUB, at + h : at + h + LANES]
                        tiles = [first(g, h) * mask, second(g, h) * mask]
                        to = g * cols + at + h
                        basis_ref[e, 2 * pair * SUB : 2 * (pair + 1) * SUB, to : to + LANES] = (
                            jnp.concatenate(tiles, 0).astype(bf16)
                        )

            def degree(s, i, j):
                def tile(g, h):
                    row = (g * DEGREES + j) * SUB
                    return held[s, i][row : row + SUB, h : h + LANES]

                return tile

            for s in range(spreads):
                for i in range(DEGREES):
                    here = (s * DEGREES + i) * cols + at
                    held[s, i] = jnp.dot(
                        row_ref[s], smooth_ref[e, :, here : here + wide], preferred_element_type=f32
                    )
                    store(s * 4 + i, degree(s, i, 0), degree(s, i, 1))
                    if i == 1:
                        store(s * 4 + 3, degree(s, 0, 2), degree(s, 1, 2))
            store(12, degree(0, 2, 2), degree(1, 2, 2))
            store(
                13,
                degree(2, 2, 2),
                lambda g, h: masked_ref[e, g * SUB : (g + 1) * SUB, at + h : at + h + LANES],
            )
        pieces = 2 if e == epochs - 1 else 1
        length = basis_ref.shape[2] // pieces
        gram = jnp.zeros((height, height), f32)
        for piece in range(pieces):
            basis = basis_ref[e, :, piece * length : (piece + 1) * length]
            product = lax.dot_general(
                basis, basis, (((1,), (1,)), ((), ())), preferred_element_type=f32
            )
            gram = gram + jnp.where(same_row, product, 0.0)
        gram = gram.reshape(planes, SUB, height).sum(1)
        gram = jnp.concatenate([gram, jnp.zeros((SLOT - planes, height), f32)], 0)
        for index, part in enumerate(split3(gram)):
            parts_ref[index, :, e * height : (e + 1) * height] = part
    system = jnp.zeros((SLOT, LANES), f32)
    for index in range(3):
        system = system + jnp.dot(parts_ref[index], place_ref[...], preferred_element_type=f32)
    plane = lax.broadcasted_iota(jnp.int32, (SLOT, LANES), 0)
    lane = lax.broadcasted_iota(jnp.int32, (SLOT, LANES), 1)
    slot = lane % SLOT
    system = system / (rows * cols) + jnp.where(plane == slot, RIDGE_TERM, 0.0)
    start = lane - slot
    column_of = [jnp.take_along_axis(system, start + l, axis=1) for l in range(NBASIS + 1)]
    direct, swapped = jnp.zeros((SLOT, LANES), f32), jnp.zeros((SLOT, LANES), f32)

    def line(l, p):
        return jnp.broadcast_to(column_of[l][p : p + 1], (SLOT, LANES))

    for p in range(0, NBASIS - 1, 2):
        q = p + 1
        a, b, d = line(p, p), line(q, p), line(q, q)
        scale = 1.0 / (a * d - b * b)
        a, b, d = a * scale, b * scale, d * scale
        outside = (plane != p) & (plane != q)
        from_p = jnp.where(outside, column_of[p] * d - column_of[q] * b, 0.0)
        from_q = jnp.where(outside, column_of[q] * a - column_of[p] * b, 0.0)
        direct = jnp.where(plane == p, d, jnp.where(plane == q, a, direct))
        swapped = jnp.where(outside, swapped, b)
        for l in range(p + 2, NBASIS + 1):
            column_of[l] = column_of[l] - from_p * line(l, p) - from_q * line(l, q)
    p = NBASIS - 1
    scale = 1.0 / line(p, p)
    direct = jnp.where(plane == p, scale, direct)
    right = column_of[NBASIS]
    right = right - jnp.where(plane != p, column_of[p] * scale, 0.0) * line(NBASIS, p)
    above, below = pltpu.roll(right, SLOT - 1, 0), pltpu.roll(right, 1, 0)
    solved = direct * right - swapped * jnp.where(plane % 2 == 0, above, below)
    natural = natural_ref[...].astype(f32)
    fold = (
        lax.broadcasted_iota(jnp.int32, (SLOT, height), 0)
        == lax.broadcasted_iota(jnp.int32, (SLOT, height), 1) // SUB
    ).astype(f32)
    sub = lax.broadcasted_iota(jnp.int32, (SUB, height), 0)
    of_row = lax.broadcasted_iota(jnp.int32, (SUB, height), 1) % SUB
    for e in range(epochs):
        column = jnp.broadcast_to(solved[:, e * SLOT : e * SLOT + 1], (SLOT, LANES))
        coefs_ref[e : e + 1, :] = jnp.sum(natural * column[:, :SLOT], 0, keepdims=True)[:, :NBASIS]
        column = jnp.where(plane < NBASIS, -column, jnp.where(plane == NBASIS, 1.0, 0.0))
        column = jnp.concatenate([column, column], 1)[:, :height]
        spread = jnp.sum(fold * column, 0, keepdims=True)
        left = jnp.where(sub == of_row, jnp.broadcast_to(spread, (SUB, height)), 0.0)
        high, middle, low = split3(left)
        left = jnp.concatenate([high, middle, low, jnp.zeros_like(low)], 0)
        target = select_ref[e]
        scale = [jnp.broadcast_to(column[k : k + 1, :LANES], (SUB, LANES)) for k in range(NBASIS)]
        for g in range(6):
            value = jnp.dot(
                left, basis_ref[e, :, g * cols : (g + 1) * cols], preferred_element_type=f32
            )
            value = value[:SUB] + (value[SUB : 2 * SUB] + value[2 * SUB : 3 * SUB])
            here = (target, slice(g * SUB, (g + 1) * SUB))
            sums_ref[here] = sums_ref[here] + value
        for g in range(6, groups):
            for b in range(blocks):
                to = g * cols + b * LANES
                tile = basis_ref[e, :, to : to + LANES].astype(f32)
                value = tile[NBASIS * SUB :]
                for k in range(NBASIS):
                    value = value + scale[k] * tile[k * SUB : (k + 1) * SUB]
                here = (target, slice(g * SUB, (g + 1) * SUB), slice(b * LANES, (b + 1) * LANES))
                sums_ref[here] = sums_ref[here] + value
    swap_sum_ref[...] = sums_ref[6:10].astype(bf16)


def between_cores(block):
    n = lax.axis_size(AXIS)
    return lax.ppermute(block, AXIS, [(i, i ^ 1) for i in range(n)])


def between_chips(block, distance):
    chips = lax.axis_size(AXIS) // CORES
    route = []
    for chip in range(chips):
        for core in range(CORES):
            origin = chip + (distance if core == 0 else -distance)
            if 0 <= origin < chips:
                route.append((CORES * origin + core, CORES * chip + core))
            else:
                route.append((CORES * chip + 1 - core, CORES * chip + core))
    return lax.ppermute(block, AXIS, route)


def buffer_of(epoch_patch):
    device = lax.axis_index(AXIS)
    core = device % CORES
    chip_offset = epoch_patch // CORES - device // CORES
    same_core = epoch_patch % CORES == core
    side = jnp.where(core == 0, 1, -1)
    far = jnp.abs(chip_offset) - 1
    mine = 2 + 2 * far + jnp.where(same_core, 0, 1)
    theirs = 6 + 2 * far + jnp.where(same_core, 1, 0)
    lean = jnp.where(far == 0, -side, side)
    away = jnp.where(chip_offset * lean > 0, mine, theirs)
    return jnp.where(chip_offset == 0, jnp.where(same_core, 0, 1), away).astype(jnp.int32)


def shards(templates, epoch_patch, images, good_pixels):
    epochs, rows, cols = images.shape
    f32, bf16 = jnp.float32, jnp.bfloat16
    assert templates.shape[0] == 1 and epochs * SLOT <= LANES
    assert lax.axis_size(AXIS) % CORES == 0 and cols % LANES == 0 and rows % SUB == 0
    other = between_cores(templates)
    pair = jnp.concatenate([templates, other], 0)
    near, far = between_chips(pair, -1), between_chips(pair, 2)
    swapped_near, swapped_far = between_cores(near), between_cores(far)
    taps = kernel_taps()
    height = (NBASIS + 1) * SUB
    tiles = epochs * (cols // LANES) * rows
    vmem, vmem_spec = pltpu.VMEM, pl.BlockSpec(memory_space=pltpu.VMEM)
    constants = (column_bands(taps), row_bands(taps, rows)) + plane_maps(epochs)
    sources = (images, good_pixels, *(jnp.asarray(c) for c in constants))
    prepared = pl.pallas_call(
        prepare_kernel,
        out_shape=[vmem((epochs, rows, cols), f32)] * 2 + [vmem(c.shape, bf16) for c in constants],
        in_specs=[pl.BlockSpec(memory_space=pltpu.HBM)] * (2 + len(constants)),
        out_specs=[vmem_spec] * (2 + len(constants)),
        scratch_shapes=[
            vmem(images.shape, bf16),
            vmem(good_pixels.shape, jnp.int32),
            pltpu.SemaphoreType.DMA((2 + len(constants),)),
        ],
        compiler_params=pltpu.CompilerParams(vmem_limit_bytes=4 << 20),
        name="prepare",
    )(*(pltpu.with_memory_space_constraint(x, pltpu.HBM) for x in sources))
    operands = (pair, near, far, swapped_near, swapped_far, *prepared)
    coefs, sums, swap_sum = pl.pallas_call(
        fit_kernel,
        out_shape=(
            vmem((epochs, NBASIS), f32),
            vmem((10, rows, cols), f32),
            vmem((4, rows, cols), bf16),
        ),
        in_specs=[pl.BlockSpec(memory_space=pltpu.SMEM)] + [vmem_spec] * len(operands),
        out_specs=[vmem_spec] * 3,
        scratch_shapes=[
            vmem((tiles, 2 * LANES), bf16),
            vmem((epochs, rows, taps.shape[0] * cols), bf16),
            vmem((epochs, height, rows // SUB * cols), bf16),
            vmem((3, SLOT, epochs * height), bf16),
        ],
        compiler_params=pltpu.CompilerParams(vmem_limit_bytes=32 << 20),
        name="fit",
    )(
        buffer_of(epoch_patch),
        *(pltpu.with_memory_space_constraint(x, pltpu.VMEM) for x in operands),
    )
    received = between_cores(swap_sum)
    near_sum = (sums[2:4] + received[0:2].astype(f32)).astype(bf16)
    far_sum = (sums[4:6] + received[2:4].astype(f32)).astype(bf16)
    near_back, far_back = between_chips(near_sum, 1), between_chips(far_sum, -2)
    total = sums[0:2] + near_back.astype(f32) + far_back.astype(f32)
    deep_sum = total[0:1] + between_cores(total[1:2].astype(bf16)).astype(f32)
    return (deep_sum, coefs)


def solution(mesh):
    spec = P(("tract", AXIS), None, None)
    in_specs = (spec, P(("tract", AXIS)), spec, spec)
    out_specs = (spec, P(("tract", AXIS), None))
    return jax.shard_map(shards, mesh=mesh, in_specs=in_specs, out_specs=out_specs, check_vma=False)
```
